256 devices in a mesh: group: 16 (over z_hi, x, core), dp: 16 (over z_lo, y).
Axes of the slice: x: 4, y: 4, z: 8 (z_hi: 2, z_lo: 4; z = z_hi * 4 + z_lo), core: 2. Of those that a mesh axis runs over, the one named last changes fastest.
Arguments:
- query_hidden: bfloat16 [2048, 32, 768], P(('dp', 'group')), may hold values from -6 to 6
- passage_hidden: bfloat16 [4096, 128, 768], P(('dp', 'group')), may hold values from -6 to 6
- projection: bfloat16 [768, 128], replicated, may hold values from -0.21875 to 0.21875
- positive: int32 [2048], P(('dp', 'group')), may hold values from 0 to 255
- hard_ids: int32 [2048, 32], P(('dp', 'group')), may hold values from -1 to 255, as said below
- passage_len: int32 [4096], P(('dp', 'group')), may hold values from 16 to 128, as said below
Outputs:
- losses: float32 [2048], P(('dp', 'group'))
- grad_proj: float32 [768, 128], replicated
- grad_query: bfloat16 [2048, 32, 768], P(('dp', 'group'))
- grad_passage: bfloat16 [4096, 128, 768], P(('dp', 'group'))
The draws below stay inside these ranges and needn't reach their ends.
Inputs may be any that keep to these rules, and one draw needn't show every extreme that they name: A passage's first passage_len tokens are live, the rest padding. `hard_ids`: A query's filled slots come first, from 8 to 32 of them; the rest hold -1. Slots may repeat a passage or name the positive.
All inputs are finite; a program needn't handle non-finite values.
Results may differ from the reference program's by a relative error of at most 0.017.
Values may be sent and summed in bfloat16 or wider, within the bound.
A program may use at most 64 MiB of HBM per device.

```python
import jax
import jax.numpy as jnp
from jax import lax

H = 768
DIM = 128
QTOK = 32
PTOK = 128
NHARD = 32
QUERY_DEV = 8
POOL = 256
QUERIES = 2048
PASSAGES = 4096
N_GROUP = 16
N_DP = 16


def draw_passage_len(key, part):
    index = jnp.arange(PASSAGES, dtype=jnp.int32)
    lowest = PTOK // 8 + (PTOK - PTOK // 8) * index // (PASSAGES - 1)
    highest = jnp.minimum(PTOK, 2 * lowest)
    raw = jax.random.randint(key, (PASSAGES,), 0, 1 << 20, dtype=jnp.int32)
    drawn = lowest + raw % (highest + 1 - lowest)
    drawn = jnp.where(index == 0, PTOK // 8, drawn)
    return jnp.where(index == PASSAGES - 1, PTOK, drawn).astype(jnp.int32)


def draw_hard_ids(key, part):
    index = jnp.arange(QUERIES, dtype=jnp.int32)
    member = index // QUERY_DEV % N_GROUP
    fewest = NHARD // 4
    filled = fewest + (NHARD - fewest) * member // max(N_GROUP - 1, 1)
    picked = jax.random.randint(jax.random.fold_in(key, 7), (QUERIES, NHARD), 0, POOL, dtype=jnp.int32)
    slot = jnp.arange(NHARD, dtype=jnp.int32)
    return jnp.where(slot[None, :] < filled[:, None], picked, -1).astype(jnp.int32)


def touch_ends(values, stream_key, least, largest):
    place = [jax.random.randint(jax.random.fold_in(stream_key, axis), (), 0, length) for axis, length in enumerate(values.shape)]
    longest = values.shape.index(max(values.shape))
    beside = place[:longest] + [(place[longest] + 1) % values.shape[longest]] + place[longest + 1:]
    return values.at[tuple(place)].set(least).at[tuple(beside)].set(largest)


def shard_levels(own_key, dims, shards, least, largest):
    def one(position, parts):
        draws = jax.random.uniform(jax.random.fold_in(jax.random.fold_in(own_key, 6), position), (parts,), jnp.float32, least / len(shards), largest / len(shards))
        return jnp.repeat(jnp.exp(draws), dims[position] // parts).reshape((-1,) + (1,) * (len(dims) - position - 1))

    loudness = one(*shards[0])
    for cut in shards[1:]:
        loudness = loudness * one(*cut)
    return loudness


def noise(own_key, dims, width, reach, pieces=(), held_as=jnp.bfloat16):
    values = jax.random.normal(own_key, dims, jnp.float32) * width
    if len(pieces) > 0:
        values = shard_levels(own_key, dims, pieces, -0.22, 0.18) * values
    return jnp.clip(values, min=-reach, max=reach).astype(held_as)


def setup_inputs(seed: int = 0) -> dict:
    streams_of = jax.random.split(jax.random.key(seed), 7)
    query_hidden = noise(streams_of[0], (QUERIES, QTOK, H), 1.0, 6.0, ((0, 256),))
    passage_hidden = noise(streams_of[1], (PASSAGES, PTOK, H), 1.0, 6.0, ((0, 256),))
    projection = noise(streams_of[2], (H, DIM), H ** -0.5, 0.21875)
    positive = touch_ends(jax.random.randint(streams_of[3], (QUERIES,), 0, POOL), jax.random.fold_in(streams_of[3], 1), 0, POOL - 1).astype(jnp.int32)
    hard_ids = draw_hard_ids(jax.random.fold_in(streams_of[6], 71), 0)
    passage_len = draw_passage_len(jax.random.fold_in(streams_of[6], 71), 0)
    return {"query_hidden": query_hidden, "passage_hidden": passage_hidden, "projection": projection, "positive": positive, "hard_ids": hard_ids, "passage_len": passage_len}


smooth_temp = 0.1
norm_eps = 1e-06

def normalize(projected):
    return projected * lax.rsqrt(lax.optimization_barrier(jnp.sum(projected * projected, axis=-1, keepdims=True)) + norm_eps)

def contract_last(left, right):
    return lax.dot_general(left, right, (((1,), (1,)), ((), ())), preferred_element_type=jnp.float32)

def contract_first(left, right):
    return lax.dot_general(left, right, (((0,), (0,)), ((), ())), preferred_element_type=jnp.float32)

def smooth_scores(query_rows, passage_rows, usable):
    similar = contract_last(query_rows, passage_rows)
    similar = similar.reshape(similar.shape[0], usable.shape[0], usable.shape[1])
    summed = lax.optimization_barrier(jnp.sum(jnp.where(usable[None], jnp.exp(similar / smooth_temp), 0.0), axis=-1))
    return smooth_temp * jnp.log(summed)

def token_grads(query_rows, passage_rows, usable, smooth, weights):
    similar = contract_last(query_rows, passage_rows)
    similar = similar.reshape(similar.shape[0], usable.shape[0], usable.shape[1])
    shares = jnp.where(usable[None], jnp.exp(similar / smooth_temp - smooth[:, :, None] / smooth_temp), 0.0)
    coefficient = (weights[:, :, None] * shares).astype(jnp.bfloat16)
    coefficient = coefficient.reshape(query_rows.shape[0], passage_rows.shape[0])
    query_part = jnp.dot(coefficient, passage_rows, preferred_element_type=jnp.float32)
    passage_part = contract_first(coefficient, query_rows)
    return (query_part, passage_part)

def hard_counts(hard_ids, pool_size):
    columns = jnp.arange(pool_size, dtype=jnp.int32)
    return lax.optimization_barrier(jnp.sum((hard_ids[:, :, None] == columns[None, None, :]).astype(jnp.float32), axis=1))

def finish_loss(scores, positive, counts, hard_mean, boost):
    columns = jnp.arange(scores.shape[1], dtype=jnp.int32)
    chosen = positive[:, None] == columns[None, :]
    pos_score = lax.optimization_barrier(jnp.sum(jnp.where(chosen, scores, 0.0), axis=1, keepdims=True))
    reweight = 1.0 + jnp.where(chosen, 0.0, boost * counts * jnp.exp(scores - jnp.log(hard_mean)))
    weighted = reweight * jnp.exp(scores - pos_score)
    partition = lax.optimization_barrier(jnp.sum(weighted, axis=1, keepdims=True))
    losses = jnp.log(partition[:, 0])
    score_grad = weighted / partition - chosen.astype(jnp.float32)
    return (losses, score_grad)

def reference(query_hidden, passage_hidden, projection, positive, hard_ids, passage_len):
    query_flat = query_hidden.reshape(QUERIES * QTOK, H)
    passage_flat = passage_hidden.reshape(PASSAGES * PTOK, H)
    query_pre = jnp.dot(query_flat, projection, preferred_element_type=jnp.float32)
    passage_pre = jnp.dot(passage_flat, projection, preferred_element_type=jnp.float32)
    query_embed = normalize(query_pre).astype(jnp.bfloat16)
    passage_embed = normalize(passage_pre).astype(jnp.bfloat16)
    usable = jnp.arange(PTOK, dtype=jnp.int32)[None, :] < passage_len[:, None]
    block_rows = QUERY_DEV * QTOK
    query_pools = query_embed.reshape(N_DP, N_GROUP, block_rows, DIM)
    passage_pools = passage_embed.reshape(N_DP, POOL * PTOK, DIM)
    usable_pools = usable.reshape(N_DP, POOL, PTOK)

    def forward_pool(members):
        query_blocks, passage_rows, usable_rows = members
        return lax.map(lambda query_block: smooth_scores(query_block, passage_rows, usable_rows), query_blocks)
    smooth = lax.map(forward_pool, (query_pools, passage_pools, usable_pools))
    scores = lax.optimization_barrier(jnp.sum(smooth.reshape(QUERIES, QTOK, POOL), axis=1))
    counts = hard_counts(hard_ids, POOL)
    hard_mean = jnp.sum(counts * jnp.exp(scores)) / (QUERIES * NHARD)
    losses, score_grad = finish_loss(scores, positive, counts, hard_mean, POOL / NHARD)
    weights = jnp.repeat(score_grad, QTOK, axis=0).reshape(N_DP, N_GROUP, block_rows, POOL)
    smooth_pools = smooth.reshape(N_DP, N_GROUP, block_rows, POOL)

    def backward_pool(members):
        query_blocks, passage_rows, usable_rows, smooth_blocks, weight_blocks = members

        def step_block(running, inner):
            query_part, passage_part = token_grads(inner[0], passage_rows, usable_rows, inner[1], inner[2])
            rounded = lax.optimization_barrier(passage_part.astype(jnp.bfloat16))
            return (running + rounded.astype(jnp.float32), query_part)
        initial = jnp.zeros((POOL * PTOK, DIM), jnp.float32)
        return lax.scan(step_block, initial, (query_blocks, smooth_blocks, weight_blocks))
    passage_grad, query_grad = lax.map(backward_pool, (query_pools, passage_pools, usable_pools, smooth_pools, weights))
    query_grad = query_grad.reshape(QUERIES * QTOK, DIM)
    passage_grad = passage_grad.reshape(PASSAGES * PTOK, DIM)
    query_back = jax.vjp(normalize, query_pre)[1](query_grad)[0].astype(jnp.bfloat16)
    passage_back = jax.vjp(normalize, passage_pre)[1](passage_grad)[0].astype(jnp.bfloat16)
    grad_query = contract_last(query_back, projection).astype(jnp.bfloat16).reshape(QUERIES, QTOK, H)
    grad_passage = contract_last(passage_back, projection).astype(jnp.bfloat16).reshape(PASSAGES, PTOK, H)
    grad_proj = contract_first(query_flat, query_back) + contract_first(passage_flat, passage_back)
    return (losses, grad_proj, grad_query, grad_passage)
```

```python
import functools

import jax
import jax.numpy as jnp
from jax import lax
from jax.experimental import pallas as pl
from jax.experimental.pallas import tpu as pltpu
from jax.sharding import Mesh
from jax.sharding import PartitionSpec as P

MESH = pl.DeviceIdType.MESH
F32 = jnp.float32
BF16 = jnp.bfloat16

AXES = ("zh", "x", "c", "zl", "y")
SPLIT = ("zl", "y", "zh", "x", "c")
norm_eps = 1e-06
EXP2_SCALE = 14.426950408889634
SHIFT = 12.0
HIGHEST = lax.Precision.HIGHEST

GROUP_RELATIVE = [(dz, dx, dc) for dz in range(2) for dx in range(4) for dc in range(2)]


def slot_of(dz, dx, dc):
    return dz * 8 + dx * 2 + dc


def back(d, n):
    return (n - d) % n


def contract_last(left, right):
    return lax.dot_general(
        left, right, (((1,), (1,)), ((), ())), preferred_element_type=F32
    )


def norm_vjp(pre, grad):
    scale = lax.rsqrt(jnp.sum(pre * pre, axis=-1, keepdims=True) + norm_eps)
    along = jnp.sum(pre * grad, axis=-1, keepdims=True)
    return scale * grad - pre * (scale * scale * scale * along)


class Sems:
    def __init__(self):
        self.total = 0

    def take(self, count):
        first = self.total
        self.total += count
        return first


SEND = Sems()
RECV = Sems()
LOCAL = Sems()
S_GATHER, R_GATHER = SEND.take(15), RECV.take(16)
S_META, R_META = SEND.take(16), RECV.take(16)
S_STATS, R_STATS = SEND.take(16), RECV.take(16)
S_HARD, R_HARD = SEND.take(16), RECV.take(16)
S_QC, R_QC = SEND.take(8), RECV.take(8)
S_QX, R_QX = SEND.take(8), RECV.take(8)
S_QZ, R_QZ = SEND.take(1), RECV.take(1)
S_AC, R_AC = SEND.take(1), RECV.take(1)
S_AX, R_AX = SEND.take(4), RECV.take(4)
S_AY, R_AY = SEND.take(4), RECV.take(4)
S_AZ, R_AZ = SEND.take(8), RECV.take(8)
S_GY, R_GY = SEND.take(4), RECV.take(4)
S_GX, R_GX = SEND.take(4), RECV.take(4)
S_GC, R_GC = SEND.take(1), RECV.take(1)
P_CHUNKS = 4
L_IN = LOCAL.take(P_CHUNKS)
L_OUT = LOCAL.take(P_CHUNKS)


def kernel(
    plen,
    positive,
    query_hidden,
    passage_hbm,
    projection,
    hard_ids,
    losses_out,
    proj_out,
    gq_out,
    gp_hbm,
    ph,
    q_pre,
    p_pre,
    pe,
    pe_t,
    qh_t,
    qg,
    e_ref,
    sums,
    w_ref,
    pg,
    meta,
    meta_rows,
    counts_ref,
    chosen_ref,
    score_ref,
    st_send,
    st_recv,
    h_send,
    h_recv,
    qgt,
    rc,
    cs,
    own_c,
    rx,
    zs,
    rz,
    pb_t,
    gp_buf,
    w_loc,
    ac_recv,
    h_core,
    ax_recv,
    h_x,
    ay_recv,
    h_y,
    az_recv,
    fin,
    ssem,
    rsem,
    lsem,
):
    zh, x, c = lax.axis_index("zh"), lax.axis_index("x"), lax.axis_index("c")
    zl, y = lax.axis_index("zl"), lax.axis_index("y")
    z = zh * 4 + zl

    def at_x(d):
        return {"x": lax.rem(x + d, 4)}

    def at_y(d):
        return {"y": lax.rem(y + d, 4)}

    def at_z(d):
        there = lax.rem(z + d, 8)
        return {"zh": there // 4, "zl": lax.rem(there, 4)}

    def in_group(dz, dx, dc):
        return {"zh": lax.rem(zh + dz, 2), "x": lax.rem(x + dx, 4), "c": lax.rem(c + dc, 2)}

    def in_dp(dl, dy):
        return {"zl": lax.rem(zl + dl, 4), "y": lax.rem(y + dy, 4)}

    partner = {"c": 1 - c}
    across = {"zh": 1 - zh}

    def group_of(dz, dx, dc):
        return (lax.rem(zh + dz, 2) * 4 + lax.rem(x + dx, 4)) * 2 + lax.rem(c + dc, 2)

    def push(src, dst, s, r, device):
        pltpu.make_async_remote_copy(
            src_ref=src,
            dst_ref=dst,
            send_sem=ssem.at[s],
            recv_sem=rsem.at[r],
            device_id=device,
            device_id_type=MESH,
        ).start()

    def arrived(dst, r):
        pltpu.make_async_remote_copy(
            src_ref=dst,
            dst_ref=dst,
            send_sem=ssem.at[0],
            recv_sem=rsem.at[r],
            device_id=partner,
            device_id_type=MESH,
        ).wait_recv()

    def sent(src, s):
        pltpu.make_async_remote_copy(
            src_ref=src,
            dst_ref=src,
            send_sem=ssem.at[s],
            recv_sem=rsem.at[0],
            device_id=partner,
            device_id_type=MESH,
        ).wait_send()

    rows_in = ph.shape[0] // P_CHUNKS

    def load(k):
        at = pl.ds(k * rows_in, rows_in)
        return pltpu.make_async_copy(passage_hbm.at[at], ph.at[at], lsem.at[L_IN + k])

    def unload(k):
        at = pl.ds(k * rows_in, rows_in)
        return pltpu.make_async_copy(gp_buf.at[at], gp_hbm.at[at], lsem.at[L_OUT + k])

    for k in range(P_CHUNKS):
        load(k).start()

    barrier = pltpu.get_barrier_semaphore()
    peers = [in_group(*r) for r in GROUP_RELATIVE[1:]]
    peers += [in_dp(dl, dy) for dl in range(4) for dy in range(4) if (dl, dy) != (0, 0)]
    peers += [{"zh": 1 - zh, "zl": lax.rem(zl + d, 4)} for d in range(1, 4)]
    for peer in peers:
        pl.semaphore_signal(barrier, inc=1, device_id=peer, device_id_type=MESH)

    pre = jnp.dot(query_hidden[...], projection[...], preferred_element_type=F32)
    q_pre[...] = pre
    scale = lax.rsqrt(jnp.sum(pre * pre, axis=-1, keepdims=True) + norm_eps)
    qg[0] = (pre * scale).astype(BF16)

    lanes = lax.broadcasted_iota(jnp.int32, (8, 128), 1)
    rows = lax.broadcasted_iota(jnp.int32, (8, 128), 0)
    chosen_row = jnp.zeros((8, 128), F32)
    for k in range(8):
        chosen_row = jnp.where(rows == k, positive[k].astype(F32), chosen_row)
    meta[0] = jnp.where(lanes == 32, chosen_row, 0.0)
    meta[0, :, 0:32] = hard_ids[...].astype(F32)

    pl.semaphore_wait(barrier, len(peers))

    push(qg.at[0], qg.at[slot_of(1, 0, 0)], S_GATHER, R_GATHER + slot_of(1, 0, 0), across)
    for n, d in enumerate((2, 1, 3)):
        to = slot_of(0, back(d, 4), 0)
        push(qg.at[0], qg.at[to], S_GATHER + 1 + n, R_GATHER + to, at_x(d))
    push(qg.at[0], qg.at[1], S_GATHER + 4, R_GATHER + 1, partner)
    for dz, dx, dc in GROUP_RELATIVE[1:]:
        to = slot_of(dz, back(dx, 4), dc)
        push(
            meta.at[0],
            meta.at[to],
            S_META + slot_of(dz, dx, dc),
            R_META + to,
            in_group(dz, dx, dc),
        )

    for k in range(P_CHUNKS):
        load(k).wait()
        at = pl.ds(k * rows_in, rows_in)
        pre = jnp.dot(ph[at, :], projection[...], preferred_element_type=F32)
        p_pre[at, :] = pre
        scale = lax.rsqrt(jnp.sum(pre * pre, axis=-1, keepdims=True) + norm_eps)
        unit = (pre * scale).astype(BF16)
        pe[at, :] = unit
        pe_t[:, at] = unit.T
    qh_t[...] = query_hidden[...].T

    def relay_x(dz, first):
        for n, d in enumerate((1, 2, 3)):
            here, there = slot_of(dz, d, 0), slot_of(dz, d, 1)
            arrived(qg.at[here], R_GATHER + here)
            push(qg.at[here], qg.at[there], first + n, R_GATHER + there, partner)

    def relay_z():
        here = slot_of(1, 0, 0)
        arrived(qg.at[here], R_GATHER + here)
        for n, d in enumerate((2, 1, 3)):
            to = slot_of(1, back(d, 4), 0)
            push(qg.at[here], qg.at[to], S_GATHER + 8 + n, R_GATHER + to, at_x(d))
        push(qg.at[here], qg.at[here + 1], S_GATHER + 11, R_GATHER + here + 1, partner)

    def count_hard():
        for dz, dx, dc in GROUP_RELATIVE:
            slot = slot_of(dz, dx, dc)
            if slot:
                arrived(meta.at[slot], R_META + slot)
            first = pl.multiple_of(group_of(dz, dx, dc) * 8, 8)
            meta_rows[pl.ds(first, 8), :] = meta[slot]
        turned = meta_rows[...].T
        own = (
            group_of(0, 0, 0) * 16 + lax.broadcasted_iota(jnp.int32, (16, 128), 0)
        ).astype(F32)
        counts = jnp.zeros((16, 128), F32)
        for k in range(32):
            counts += (turned[k : k + 1, :] == own).astype(F32)
        counts_ref[...] = counts
        chosen_ref[...] = (turned[32:33, :] == own).astype(F32)

    passages = sums.shape[1]
    step = 4
    height = step * 128

    def forward(k, carry):
        @pl.when(k == 1)
        def _():
            relay_x(0, S_GATHER + 5)

        @pl.when(k == 4)
        def _():
            relay_z()

        @pl.when(k == 6)
        def _():
            count_hard()

        @pl.when(k == 10)
        def _():
            relay_x(1, S_GATHER + 12)

        @pl.when(lax.rem(k, 2) == 1)
        def _():
            arrived(qg.at[k], R_GATHER + k)

        block = qg[k]
        for n in range(passages // step):
            similar = contract_last(pe[n * height : (n + 1) * height, :], block)
            grown = jnp.exp2(similar * EXP2_SCALE)
            for i in range(step):
                p = n * step + i
                token = lax.broadcasted_iota(jnp.int32, (128, grown.shape[1]), 0)
                live = jnp.where(token < plen[p], grown[i * 128 : (i + 1) * 128], 0.0)
                e_ref[k, p * 128 : (p + 1) * 128, :] = live.astype(BF16)
                sums[k, p : p + 1, :] = jnp.sum(live, axis=0, keepdims=True)
        return carry

    lax.fori_loop(0, 16, forward, 0)

    tokens = sums.shape[2]
    every = sums[...].reshape(16 * passages, tokens)
    spread_from = (
        lax.broadcasted_iota(jnp.int32, (tokens, 128), 0) // 32
        == lax.rem(lax.broadcasted_iota(jnp.int32, (tokens, 128), 1), 8)
    ).astype(F32)
    spread_to = (
        lax.broadcasted_iota(jnp.int32, (128, tokens), 1) // 32
        == lax.rem(lax.broadcasted_iota(jnp.int32, (128, tokens), 0), 8)
    ).astype(F32)
    per_slot = jnp.dot(
        0.1 * jnp.log(every), spread_from, precision=HIGHEST, preferred_element_type=F32
    )
    lane_group = lax.broadcasted_iota(jnp.int32, (passages, 128), 1) // 8
    scores = jnp.zeros((passages, 128), F32)
    for dz, dx, dc in GROUP_RELATIVE:
        slot = slot_of(dz, dx, dc)
        part = per_slot[slot * passages : (slot + 1) * passages]
        scores += jnp.where(lane_group == group_of(dz, dx, dc), part, 0.0)

    counts, chosen = counts_ref[...], chosen_ref[...]
    grown = jnp.exp(scores - SHIFT)
    hard = counts * grown
    other_hard = jnp.where(chosen > 0.5, 0.0, hard)
    score_ref[...] = scores
    st_send[...] = jnp.zeros_like(st_send)
    st_send[0:1, :] = jnp.sum(grown, axis=0, keepdims=True)
    st_send[1:2, :] = jnp.sum(other_hard * grown, axis=0, keepdims=True)
    st_send[2:3, :] = jnp.sum(chosen * scores, axis=0, keepdims=True)
    st_send[3:4, :] = jnp.sum(hard, axis=0, keepdims=True)
    for dz, dx, dc in GROUP_RELATIVE[1:]:
        to = slot_of(dz, back(dx, 4), dc)
        push(
            st_send,
            st_recv.at[to],
            S_STATS + slot_of(dz, dx, dc),
            R_STATS + to,
            in_group(dz, dx, dc),
        )
    stats = st_send[...]
    for slot in range(1, 16):
        arrived(st_recv.at[slot], R_STATS + slot)
        stats += st_recv[slot]
    h_send[...] = stats
    for dl in range(4):
        for dy in range(4):
            if (dl, dy) != (0, 0):
                to = back(dl, 4) * 4 + back(dy, 4)
                push(
                    h_send,
                    h_recv.at[to],
                    S_HARD + dl * 4 + dy,
                    R_HARD + to,
                    in_dp(dl, dy),
                )
    total = stats[3:4, :]
    for slot in range(1, 16):
        arrived(h_recv.at[slot], R_HARD + slot)
        total += h_recv[slot, 3:4, :]
    boost = (8.0 * 65536.0) / jnp.sum(total, axis=1, keepdims=True)
    partition = stats[0:1, :] + boost * stats[1:2, :]
    loss = jnp.log(partition) + SHIFT - stats[2:3, :]
    own_lane = lanes == group_of(0, 0, 0) * 8 + rows
    losses_out[...] = jnp.broadcast_to(
        jnp.sum(jnp.where(own_lane, loss, 0.0), axis=1, keepdims=True), (8, 128)
    )
    score_grad = grown * (1.0 + boost * other_hard) / partition - chosen

    picked = [
        jnp.where(lane_group == group_of(dz, dx, dc), score_grad, 0.0)
        for dz, dx, dc in GROUP_RELATIVE
    ]
    spread = jnp.dot(
        jnp.concatenate(picked, axis=0),
        spread_to,
        precision=HIGHEST,
        preferred_element_type=F32,
    )
    w_ref[...] = (spread / every).reshape(w_ref.shape)
    pg[...] = jnp.zeros_like(pg)

    def combine(j):
        arrived(rc.at[j], R_QC + j)
        both = qgt[2 * j + 1].astype(F32) + rc[j].astype(F32)
        side = j // 4
        d = lax.rem(j + 1, 4)

        @pl.when(d != 0)
        def _():
            cs[j] = both.astype(BF16)
            to = side * 4 + (4 - d)
            push(cs.at[j], rx.at[to], S_QX + j, R_QX + to, {"x": lax.rem(x + d, 4)})

        @pl.when(d == 0)
        def _():
            own_c[side] = both

    def over_x(side):
        whole = own_c[side]
        for d in range(1, 4):
            arrived(rx.at[side * 4 + d], R_QX + side * 4 + d)
            whole += rx[side * 4 + d].astype(F32)
        return whole

    def backward(it, carry):
        j = it // 2
        dz = 1 - j // 4
        dx = lax.rem(j + 1, 4)
        dc = 1 - lax.rem(it, 2)
        k = dz * 8 + dx * 2 + dc
        block = qg[k]
        acc = None
        for n in range(passages // step):
            parts = []
            for i in range(step):
                p = n * step + i
                weight = w_ref[k, p : p + 1, :]
                kept = e_ref[k, p * 128 : (p + 1) * 128, :].astype(F32)
                parts.append((kept * weight).astype(BF16))
            coefficient = jnp.concatenate(parts, axis=0)
            at = slice(n * height, (n + 1) * height)
            pg[at, :] += jnp.dot(coefficient, block, preferred_element_type=F32)
            term = jnp.dot(pe_t[:, at], coefficient, preferred_element_type=F32)
            acc = term if acc is None else acc + term
        qgt[it] = acc.astype(BF16)

        @pl.when(dc == 1)
        def _():
            push(qgt.at[it], rc.at[j], S_QC + j, R_QC + j, partner)

            @pl.when(it >= 2)
            def _():
                combine(j - 1)

        @pl.when(it == 13)
        def _():
            zs[...] = over_x(0).astype(BF16)
            push(zs, rz, S_QZ, R_QZ, across)

        return carry

    lax.fori_loop(0, 16, backward, 0)
    combine(7)

    w_t = jnp.zeros((128, ph.shape[1]), F32)
    for k in range(P_CHUNKS):
        at = pl.ds(k * rows_in, rows_in)
        pb = norm_vjp(p_pre[at, :], pg[at, :]).astype(BF16)
        pb_t[:, at] = pb.T
        gp_buf[at, :] = contract_last(pb, projection[...]).astype(BF16)
        unload(k).start()
    w_t = jnp.dot(pb_t[...], ph[...], preferred_element_type=F32)
    w_loc[...] = w_t.T

    arrived(rz, R_QZ)
    whole = over_x(1) + rz[...].astype(F32)
    qb = norm_vjp(q_pre[...], whole.T).astype(BF16)
    w_loc[...] += jnp.dot(qh_t[...], qb, preferred_element_type=F32)

    half = w_loc.shape[0] // 2
    quarter = half // 4
    piece = quarter // 4

    def rows_at(first, count):
        return pl.ds(pl.multiple_of(first, 8), count)

    push(w_loc.at[rows_at((1 - c) * half, half)], ac_recv, S_AC, R_AC, partner)
    gq_out[...] = contract_last(qb, projection[...]).astype(BF16)
    arrived(ac_recv, R_AC)
    h_core[...] = w_loc[rows_at(c * half, half), :] + ac_recv[...]
    for d in (2, 1, 3):
        push(
            h_core.at[rows_at(lax.rem(x + d, 4) * quarter, quarter)],
            ax_recv.at[4 - d],
            S_AX + d,
            R_AX + 4 - d,
            at_x(d),
        )
    mine = h_core[rows_at(x * quarter, quarter), :]
    for d in range(1, 4):
        arrived(ax_recv.at[d], R_AX + d)
        mine += ax_recv[d]
    h_x[...] = mine
    for d in (2, 1, 3):
        push(
            h_x.at[rows_at(lax.rem(y + d, 4) * piece, piece)],
            ay_recv.at[4 - d],
            S_AY + d,
            R_AY + 4 - d,
            at_y(d),
        )
    mine = h_x[rows_at(y * piece, piece), :]
    for d in range(1, 4):
        arrived(ay_recv.at[d], R_AY + d)
        mine += ay_recv[d]
    h_y[...] = mine
    for d in (4, 3, 5, 2, 6, 1, 7):
        push(h_y, az_recv.at[z], S_AZ + d, R_AZ + 8 - d, at_z(d))
    az_recv[z] = mine
    for d in range(1, 8):
        arrived(az_recv.at[0], R_AZ + d)
    mine = az_recv[0]
    for k in range(1, 8):
        mine += az_recv[k]
    base = c * half + x * quarter
    own_rows = rows_at(base + y * piece, piece)
    fin[own_rows, :] = mine
    for d in (2, 1, 3):
        push(fin.at[own_rows], fin.at[own_rows], S_GY + d, R_GY + 4 - d, at_y(d))
    for d in range(1, 4):
        arrived(fin.at[own_rows], R_GY + d)
    own_rows = rows_at(base, quarter)
    for d in (2, 1, 3):
        push(fin.at[own_rows], fin.at[own_rows], S_GX + d, R_GX + 4 - d, at_x(d))
    for d in range(1, 4):
        arrived(fin.at[own_rows], R_GX + d)
    own_rows = rows_at(c * half, half)
    push(fin.at[own_rows], fin.at[own_rows], S_GC, R_GC, partner)
    arrived(fin.at[own_rows], R_GC)
    proj_out[...] = fin[...]

    for n in range(15):
        sent(qg.at[0], S_GATHER + n)
    for n in range(1, 16):
        sent(meta.at[0], S_META + n)
        sent(st_send, S_STATS + n)
        sent(h_send, S_HARD + n)
    for n in range(8):
        sent(qgt.at[0], S_QC + n)
        if n % 4 != 3:
            sent(cs.at[0], S_QX + n)
    sent(zs, S_QZ)
    sent(ac_recv, S_AC)
    for d in range(1, 4):
        sent(ax_recv.at[0], S_AX + d)
        sent(ay_recv.at[0], S_AY + d)
        sent(h_y, S_GY + d)
        sent(h_x, S_GX + d)
    for d in range(1, 8):
        sent(h_y, S_AZ + d)
    sent(ac_recv, S_GC)
    for k in range(P_CHUNKS):
        unload(k).wait()


def local(query_hidden, passage_hidden, projection, positive, hard_ids, passage_len):
    queries, query_len, width = query_hidden.shape
    passages, slots, _ = passage_hidden.shape
    dim = projection.shape[1]
    q_rows, p_rows = queries * query_len, passages * slots
    half = width // 2
    quarter = half // 4
    piece = quarter // 4
    vmem = pl.BlockSpec(memory_space=pltpu.VMEM)
    smem = pl.BlockSpec(memory_space=pltpu.SMEM)
    hbm = pl.BlockSpec(memory_space=pl.ANY)
    scratch = [
        pltpu.VMEM((p_rows, width), BF16),
        pltpu.VMEM((q_rows, dim), F32),
        pltpu.VMEM((p_rows, dim), F32),
        pltpu.VMEM((p_rows, dim), BF16),
        pltpu.VMEM((dim, p_rows), BF16),
        pltpu.VMEM((width, q_rows), BF16),
        pltpu.VMEM((16, q_rows, dim), BF16),
        pltpu.VMEM((16, p_rows, q_rows), BF16),
        pltpu.VMEM((16, passages, q_rows), F32),
        pltpu.VMEM((16, passages, q_rows), F32),
        pltpu.VMEM((p_rows, dim), F32),
        pltpu.VMEM((16, 8, 128), F32),
        pltpu.VMEM((128, 128), F32),
        pltpu.VMEM((passages, 128), F32),
        pltpu.VMEM((passages, 128), F32),
        pltpu.VMEM((passages, 128), F32),
        pltpu.VMEM((8, 128), F32),
        pltpu.VMEM((16, 8, 128), F32),
        pltpu.VMEM((8, 128), F32),
        pltpu.VMEM((16, 8, 128), F32),
        pltpu.VMEM((16, dim, q_rows), BF16),
        pltpu.VMEM((8, dim, q_rows), BF16),
        pltpu.VMEM((8, dim, q_rows), BF16),
        pltpu.VMEM((2, dim, q_rows), F32),
        pltpu.VMEM((8, dim, q_rows), BF16),
        pltpu.VMEM((dim, q_rows), BF16),
        pltpu.VMEM((dim, q_rows), BF16),
        pltpu.VMEM((dim, p_rows), BF16),
        pltpu.VMEM((p_rows, width), BF16),
        pltpu.VMEM((width, dim), F32),
        pltpu.VMEM((half, dim), F32),
        pltpu.VMEM((half, dim), F32),
        pltpu.VMEM((4, quarter, dim), F32),
        pltpu.VMEM((quarter, dim), F32),
        pltpu.VMEM((4, piece, dim), F32),
        pltpu.VMEM((piece, dim), F32),
        pltpu.VMEM((8, piece, dim), F32),
        pltpu.VMEM((width, dim), F32),
        pltpu.SemaphoreType.DMA((SEND.total,)),
        pltpu.SemaphoreType.DMA((RECV.total,)),
        pltpu.SemaphoreType.DMA((LOCAL.total,)),
    ]
    losses, grad_proj, grad_query, grad_passage = pl.pallas_call(
        kernel,
        out_shape=(
            jax.ShapeDtypeStruct((8, 128), F32),
            jax.ShapeDtypeStruct((width, dim), F32),
            jax.ShapeDtypeStruct((q_rows, width), BF16),
            jax.ShapeDtypeStruct((p_rows, width), BF16),
        ),
        in_specs=[smem, smem, vmem, hbm, vmem, vmem],
        out_specs=(vmem, vmem, vmem, hbm),
        scratch_shapes=scratch,
        compiler_params=pltpu.CompilerParams(
            collective_id=0, has_side_effects=True, vmem_limit_bytes=60 << 20
        ),
        name="late_interaction_step",
    )(
        passage_len,
        positive,
        query_hidden.reshape(q_rows, width),
        passage_hidden.reshape(p_rows, width),
        projection,
        hard_ids,
    )
    return (
        losses[:, 0],
        grad_proj,
        grad_query.reshape(query_hidden.shape),
        grad_passage.reshape(passage_hidden.shape),
    )


def solution(mesh):
    split = Mesh(mesh.devices.reshape(2, 4, 2, 4, 4), AXES)
    placed = (
        P(SPLIT, None, None),
        P(SPLIT, None, None),
        P(),
        P(SPLIT),
        P(SPLIT, None),
        P(SPLIT),
    )
    return jax.shard_map(
        local,
        mesh=split,
        in_specs=placed,
        out_specs=(P(SPLIT), P(), P(SPLIT, None, None), P(SPLIT, None, None)),
        check_vma=False,
    )
```

```python
import functools

import jax
import jax.numpy as jnp
from jax import lax
from jax.experimental import pallas as pl
from jax.experimental.pallas import tpu as pltpu
from jax.sharding import Mesh
from jax.sharding import PartitionSpec as P

MESH = pl.DeviceIdType.MESH
F32 = jnp.float32
BF16 = jnp.bfloat16

AXES = ("zh", "x", "c", "zl", "y")
SPLIT = ("zl", "y", "zh", "x", "c")
norm_eps = 1e-06
EXP2_SCALE = 14.426950408889634
SHIFT = 12.0
HIGHEST = lax.Precision.HIGHEST

GROUP_RELATIVE = [(dz, dx, dc) for dz in range(2) for dx in range(4) for dc in range(2)]

PLANE_RELATIVE = [(dx, dc, dy) for dx in range(4) for dc in range(2) for dy in range(4)]


def slot_of(dz, dx, dc):
    return dz * 8 + dx * 2 + dc


def back(d, n):
    return (n - d) % n


def contract_last(left, right):
    return lax.dot_general(
        left, right, (((1,), (1,)), ((), ())), preferred_element_type=F32
    )


def norm_vjp(pre, grad):
    scale = lax.rsqrt(jnp.sum(pre * pre, axis=-1, keepdims=True) + norm_eps)
    along = jnp.sum(pre * grad, axis=-1, keepdims=True)
    return scale * grad - pre * (scale * scale * scale * along)


class Sems:
    def __init__(self):
        self.total = 0

    def take(self, count):
        first = self.total
        self.total += count
        return first


SEND = Sems()
RECV = Sems()
LOCAL = Sems()
S_GATHER, R_GATHER = SEND.take(15), RECV.take(16)
S_META, R_META = SEND.take(16), RECV.take(16)
S_STATS, R_STATS = SEND.take(16), RECV.take(16)
S_HARD, R_HARD = SEND.take(32), RECV.take(32)
S_HZ, R_HZ = SEND.take(8), RECV.take(8)
S_QC, R_QC = SEND.take(8), RECV.take(8)
S_QX, R_QX = SEND.take(8), RECV.take(8)
S_QZ, R_QZ = SEND.take(1), RECV.take(1)
S_AC, R_AC = SEND.take(1), RECV.take(1)
S_AX, R_AX = SEND.take(4), RECV.take(4)
S_AY, R_AY = SEND.take(4), RECV.take(4)
S_AZ, R_AZ = SEND.take(8), RECV.take(8)
S_GY, R_GY = SEND.take(4), RECV.take(4)
S_GX, R_GX = SEND.take(4), RECV.take(4)
S_GC, R_GC = SEND.take(1), RECV.take(1)
P_CHUNKS = 4
OUT_CHUNKS = 4
L_IN = LOCAL.take(P_CHUNKS)


def kernel(
    plen,
    positive,
    query_hidden,
    passage_hbm,
    projection,
    hard_ids,
    losses_out,
    fin,
    qb_out,
    pb_out,
    ph,
    q_pre,
    p_pre,
    pe,
    pe_t,
    qh_t,
    qg,
    e_ref,
    sums,
    w_ref,
    pg,
    meta,
    meta_rows,
    counts_ref,
    chosen_ref,
    score_ref,
    st_send,
    st_recv,
    h_recv,
    hz_recv,
    qgt,
    rc,
    cs,
    own_c,
    rx,
    zs,
    rz,
    pb_t,
    w_loc,
    w_send,
    ac_recv,
    h_core,
    ax_recv,
    h_x,
    ay_recv,
    h_y,
    az_recv,
    parts,
    ssem,
    rsem,
    lsem,
):
    zh, x, c = lax.axis_index("zh"), lax.axis_index("x"), lax.axis_index("c")
    zl, y = lax.axis_index("zl"), lax.axis_index("y")
    z = zh * 4 + zl

    def at_x(d):
        return {"x": lax.rem(x + d, 4)}

    def at_y(d):
        return {"y": lax.rem(y + d, 4)}

    def at_z(d):
        there = lax.rem(z + d, 8)
        return {"zh": there // 4, "zl": lax.rem(there, 4)}

    def in_group(dz, dx, dc):
        return {"zh": lax.rem(zh + dz, 2), "x": lax.rem(x + dx, 4), "c": lax.rem(c + dc, 2)}

    def in_plane(dx, dc, dy):
        return {"x": lax.rem(x + dx, 4), "c": lax.rem(c + dc, 2), "y": lax.rem(y + dy, 4)}

    partner = {"c": 1 - c}
    across = {"zh": 1 - zh}

    def group_of(dz, dx, dc):
        return (lax.rem(zh + dz, 2) * 4 + lax.rem(x + dx, 4)) * 2 + lax.rem(c + dc, 2)

    def push(src, dst, s, r, device):
        pltpu.make_async_remote_copy(
            src_ref=src,
            dst_ref=dst,
            send_sem=ssem.at[s],
            recv_sem=rsem.at[r],
            device_id=device,
            device_id_type=MESH,
        ).start()

    def arrived(dst, r):
        pltpu.make_async_remote_copy(
            src_ref=dst,
            dst_ref=dst,
            send_sem=ssem.at[0],
            recv_sem=rsem.at[r],
            device_id=partner,
            device_id_type=MESH,
        ).wait_recv()

    def sent(src, s):
        pltpu.make_async_remote_copy(
            src_ref=src,
            dst_ref=src,
            send_sem=ssem.at[s],
            recv_sem=rsem.at[0],
            device_id=partner,
            device_id_type=MESH,
        ).wait_send()

    rows_in = ph.shape[0] // P_CHUNKS

    def load(k):
        at = pl.ds(k * rows_in, rows_in)
        return pltpu.make_async_copy(passage_hbm.at[at], ph.at[at], lsem.at[L_IN + k])

    for k in range(P_CHUNKS):
        load(k).start()

    barrier = pltpu.get_barrier_semaphore()
    peers = [in_group(*r) for r in GROUP_RELATIVE[1:]]
    peers += [in_plane(*r) for r in PLANE_RELATIVE[1:] if r[2]]
    peers += [at_z(d) for d in range(1, 8) if d != 4]
    for peer in peers:
        pl.semaphore_signal(barrier, inc=1, device_id=peer, device_id_type=MESH)

    pre = jnp.dot(query_hidden[...], projection[...], preferred_element_type=F32)
    q_pre[...] = pre
    scale = lax.rsqrt(jnp.sum(pre * pre, axis=-1, keepdims=True) + norm_eps)
    qg[0] = (pre * scale).astype(BF16)

    lanes = lax.broadcasted_iota(jnp.int32, (8, 128), 1)
    rows = lax.broadcasted_iota(jnp.int32, (8, 128), 0)
    chosen_row = jnp.zeros((8, 128), F32)
    for k in range(8):
        chosen_row = jnp.where(rows == k, positive[k].astype(F32), chosen_row)
    meta[0] = jnp.where(lanes == 32, chosen_row, 0.0)
    meta[0, :, 0:32] = hard_ids[...].astype(F32)

    pl.semaphore_wait(barrier, len(peers))

    push(qg.at[0], qg.at[slot_of(1, 0, 0)], S_GATHER, R_GATHER + slot_of(1, 0, 0), across)
    for n, d in enumerate((2, 1, 3)):
        to = slot_of(0, back(d, 4), 0)
        push(qg.at[0], qg.at[to], S_GATHER + 1 + n, R_GATHER + to, at_x(d))
    push(qg.at[0], qg.at[1], S_GATHER + 4, R_GATHER + 1, partner)
    for dz, dx, dc in GROUP_RELATIVE[1:]:
        to = slot_of(dz, back(dx, 4), dc)
        push(
            meta.at[0],
            meta.at[to],
            S_META + slot_of(dz, dx, dc),
            R_META + to,
            in_group(dz, dx, dc),
        )

    for k in range(P_CHUNKS):
        load(k).wait()
        at = pl.ds(k * rows_in, rows_in)
        pre = jnp.dot(ph[at, :], projection[...], preferred_element_type=F32)
        p_pre[at, :] = pre
        scale = lax.rsqrt(jnp.sum(pre * pre, axis=-1, keepdims=True) + norm_eps)
        unit = (pre * scale).astype(BF16)
        pe[at, :] = unit
        pe_t[:, at] = unit.T
    qh_t[...] = query_hidden[...].T

    def relay_x(dz, first):
        for n, d in enumerate((1, 2, 3)):
            here, there = slot_of(dz, d, 0), slot_of(dz, d, 1)
            arrived(qg.at[here], R_GATHER + here)
            push(qg.at[here], qg.at[there], first + n, R_GATHER + there, partner)

    def relay_z():
        here = slot_of(1, 0, 0)
        arrived(qg.at[here], R_GATHER + here)
        for n, d in enumerate((2, 1, 3)):
            to = slot_of(1, back(d, 4), 0)
            push(qg.at[here], qg.at[to], S_GATHER + 8 + n, R_GATHER + to, at_x(d))
        push(qg.at[here], qg.at[here + 1], S_GATHER + 11, R_GATHER + here + 1, partner)

    def count_hard():
        for dz, dx, dc in GROUP_RELATIVE:
            slot = slot_of(dz, dx, dc)
            if slot:
                arrived(meta.at[slot], R_META + slot)
            first = pl.multiple_of(group_of(dz, dx, dc) * 8, 8)
            meta_rows[pl.ds(first, 8), :] = meta[slot]
        turned = meta_rows[...].T
        own = (
            group_of(0, 0, 0) * 16 + lax.broadcasted_iota(jnp.int32, (16, 128), 0)
        ).astype(F32)
        counts = jnp.zeros((16, 128), F32)
        for k in range(32):
            counts += (turned[k : k + 1, :] == own).astype(F32)
        counts_ref[...] = counts
        chosen_ref[...] = (turned[32:33, :] == own).astype(F32)

    passages = sums.shape[1]
    step = 4
    height = step * 128

    def grow(k):
        block = qg[k]
        for n in range(passages // step):
            similar = contract_last(pe[n * height : (n + 1) * height, :], block)
            grown = jnp.exp2(similar * EXP2_SCALE)
            for i in range(step):
                p = n * step + i
                token = lax.broadcasted_iota(jnp.int32, (128, grown.shape[1]), 0)
                live = jnp.where(token < plen[p], grown[i * 128 : (i + 1) * 128], 0.0)
                e_ref[k, p * 128 : (p + 1) * 128, :] = live.astype(BF16)
                sums[k, p : p + 1, :] = jnp.sum(live, axis=0, keepdims=True)

    grow(0)
    relay_x(0, S_GATHER + 5)
    arrived(qg.at[1], R_GATHER + 1)
    grow(1)

    def forward(t, carry):
        @pl.when(t == 2)
        def _():
            relay_z()

        @pl.when(t == 3)
        def _():
            count_hard()

        @pl.when(t == 5)
        def _():
            relay_x(1, S_GATHER + 12)

        arrived(qg.at[2 * t + 1], R_GATHER + 2 * t + 1)
        grow(2 * t)
        grow(2 * t + 1)
        return carry

    lax.fori_loop(1, 8, forward, 0)

    tokens = sums.shape[2]
    every = sums[...].reshape(16 * passages, tokens)
    spread_from = (
        lax.broadcasted_iota(jnp.int32, (tokens, 128), 0) // 32
        == lax.rem(lax.broadcasted_iota(jnp.int32, (tokens, 128), 1), 8)
    ).astype(F32)
    spread_to = (
        lax.broadcasted_iota(jnp.int32, (128, tokens), 1) // 32
        == lax.rem(lax.broadcasted_iota(jnp.int32, (128, tokens), 0), 8)
    ).astype(F32)
    per_slot = jnp.dot(
        0.1 * jnp.log(every), spread_from, precision=HIGHEST, preferred_element_type=F32
    )
    lane_group = lax.broadcasted_iota(jnp.int32, (passages, 128), 1) // 8
    scores = jnp.zeros((passages, 128), F32)
    for dz, dx, dc in GROUP_RELATIVE:
        slot = slot_of(dz, dx, dc)
        part = per_slot[slot * passages : (slot + 1) * passages]
        scores += jnp.where(lane_group == group_of(dz, dx, dc), part, 0.0)

    counts, chosen = counts_ref[...], chosen_ref[...]
    grown = jnp.exp(scores - SHIFT)
    hard = counts * grown
    other_hard = jnp.where(chosen > 0.5, 0.0, hard)
    score_ref[...] = scores
    st_send[...] = jnp.zeros_like(st_send)
    st_send[0:1, :] = jnp.sum(grown, axis=0, keepdims=True)
    st_send[1:2, :] = jnp.sum(other_hard * grown, axis=0, keepdims=True)
    st_send[2:3, :] = jnp.sum(chosen * scores, axis=0, keepdims=True)
    h_recv[0:1, :] = jnp.sum(hard, axis=0, keepdims=True)
    own = h_recv.at[pl.ds(0, 1)]
    for dx, dc, dy in PLANE_RELATIVE[1:]:
        at = dx * 8 + dc * 4 + dy
        to = back(dx, 4) * 8 + dc * 4 + back(dy, 4)
        push(own, h_recv.at[pl.ds(to, 1)], S_HARD + at, R_HARD + to, in_plane(dx, dc, dy))
    for dz, dx, dc in GROUP_RELATIVE[1:]:
        to = slot_of(dz, back(dx, 4), dc)
        push(
            st_send,
            st_recv.at[to],
            S_STATS + slot_of(dz, dx, dc),
            R_STATS + to,
            in_group(dz, dx, dc),
        )
    for n in range(1, 32):
        arrived(h_recv.at[pl.ds(n, 1)], R_HARD + n)
    hz_recv[0:1, :] = jnp.sum(h_recv[...], axis=0, keepdims=True)
    own = hz_recv.at[pl.ds(0, 1)]
    for d in (4, 3, 5, 2, 6, 1, 7):
        push(own, hz_recv.at[pl.ds(8 - d, 1)], S_HZ + d, R_HZ + 8 - d, at_z(d))
    stats = st_send[...]
    for slot in range(1, 16):
        arrived(st_recv.at[slot], R_STATS + slot)
        stats += st_recv[slot]
    for n in range(1, 8):
        arrived(hz_recv.at[pl.ds(n, 1)], R_HZ + n)
    total = jnp.sum(hz_recv[...], axis=0, keepdims=True)
    boost = (8.0 * 65536.0) / jnp.sum(total, axis=1, keepdims=True)
    partition = stats[0:1, :] + boost * stats[1:2, :]
    loss = jnp.log(partition) + SHIFT - stats[2:3, :]
    own_lane = lanes == group_of(0, 0, 0) * 8 + rows
    losses_out[...] = jnp.broadcast_to(
        jnp.sum(jnp.where(own_lane, loss, 0.0), axis=1, keepdims=True), (8, 128)
    )
    score_grad = grown * (1.0 + boost * other_hard) / partition - chosen

    picked = [
        jnp.where(lane_group == group_of(dz, dx, dc), score_grad, 0.0)
        for dz, dx, dc in GROUP_RELATIVE
    ]
    spread = jnp.dot(
        jnp.concatenate(picked, axis=0),
        spread_to,
        precision=HIGHEST,
        preferred_element_type=F32,
    )
    w_ref[...] = (spread / every).reshape(w_ref.shape)
    pg[...] = jnp.zeros_like(pg)

    def combine(j):
        arrived(rc.at[j], R_QC + j)
        both = qgt[2 * j + 1].astype(F32) + rc[j].astype(F32)
        side = j // 4
        d = lax.rem(j + 1, 4)

        @pl.when(d != 0)
        def _():
            cs[j] = both.astype(BF16)
            to = side * 4 + (4 - d)
            push(cs.at[j], rx.at[to], S_QX + j, R_QX + to, {"x": lax.rem(x + d, 4)})

        @pl.when(d == 0)
        def _():
            own_c[side] = both

    def over_x(side):
        whole = own_c[side]
        for d in range(1, 4):
            arrived(rx.at[side * 4 + d], R_QX + side * 4 + d)
            whole += rx[side * 4 + d].astype(F32)
        return whole

    def backward(it, carry):
        j = it // 2
        dz = 1 - j // 4
        dx = lax.rem(j + 1, 4)
        dc = 1 - lax.rem(it, 2)
        k = dz * 8 + dx * 2 + dc
        block = qg[k]
        acc = None
        for n in range(passages // step):
            parts = []
            for i in range(step):
                p = n * step + i
                weight = w_ref[k, p : p + 1, :]
                kept = e_ref[k, p * 128 : (p + 1) * 128, :].astype(F32)
                parts.append((kept * weight).astype(BF16))
            coefficient = jnp.concatenate(parts, axis=0)
            at = slice(n * height, (n + 1) * height)
            pg[at, :] += jnp.dot(coefficient, block, preferred_element_type=F32)
            term = jnp.dot(pe_t[:, at], coefficient, preferred_element_type=F32)
            acc = term if acc is None else acc + term
        qgt[it] = acc.astype(BF16)

        @pl.when(dc == 1)
        def _():
            push(qgt.at[it], rc.at[j], S_QC + j, R_QC + j, partner)

            @pl.when(it >= 2)
            def _():
                combine(j - 1)

        @pl.when(it == 13)
        def _():
            zs[...] = over_x(0).astype(BF16)
            push(zs, rz, S_QZ, R_QZ, across)

        return carry

    lax.fori_loop(0, 16, backward, 0)
    combine(7)

    for k in range(P_CHUNKS):
        at = pl.ds(k * rows_in, rows_in)
        pb = norm_vjp(p_pre[at, :], pg[at, :]).astype(BF16)
        pb_t[:, at] = pb.T
        pb_out[at, :] = pb
    w_t = jnp.dot(pb_t[...], ph[...], preferred_element_type=F32)
    w_loc[...] = w_t.T

    arrived(rz, R_QZ)
    whole = over_x(1) + rz[...].astype(F32)
    qb = norm_vjp(q_pre[...], whole.T).astype(BF16)
    qb_out[...] = qb
    whole = w_loc[...] + jnp.dot(qh_t[...], qb, preferred_element_type=F32)
    w_loc[...] = whole
    w_send[...] = whole.astype(BF16)

    half = w_loc.shape[0] // 2
    quarter = half // 4
    piece = quarter // 4

    def rows_at(first, count):
        return pl.ds(pl.multiple_of(first, 8), count)

    push(w_send.at[rows_at((1 - c) * half, half)], ac_recv, S_AC, R_AC, partner)
    arrived(ac_recv, R_AC)
    mine = w_loc[rows_at(c * half, half), :] + ac_recv[...].astype(F32)
    w_loc[rows_at(c * half, half), :] = mine
    h_core[...] = mine.astype(BF16)
    for d in (2, 1, 3):
        push(
            h_core.at[rows_at(lax.rem(x + d, 4) * quarter, quarter)],
            ax_recv.at[4 - d],
            S_AX + d,
            R_AX + 4 - d,
            at_x(d),
        )
    base = c * half + x * quarter
    mine = w_loc[rows_at(base, quarter), :]
    for d in (1, 3, 2):
        arrived(ax_recv.at[d], R_AX + d)
        mine += ax_recv[d].astype(F32)
    h_x[...] = mine
    for d in (2, 1, 3):
        push(
            h_x.at[rows_at(lax.rem(y + d, 4) * piece, piece)],
            ay_recv.at[4 - d],
            S_AY + d,
            R_AY + 4 - d,
            at_y(d),
        )
    mine = h_x[rows_at(y * piece, piece), :]
    for d in (1, 3, 2):
        arrived(ay_recv.at[d], R_AY + d)
        mine += ay_recv[d]
    h_y[...] = mine.astype(BF16)
    for d in (4, 3, 5, 2, 6, 1, 7):
        push(h_y, az_recv.at[z], S_AZ + d, R_AZ + 8 - d, at_z(d))
    az_recv[z] = h_y[...]
    for d in range(1, 8):
        arrived(az_recv.at[0], R_AZ + d)
    mine = az_recv[0].astype(F32)
    for k in range(1, 8):
        mine += az_recv[k].astype(F32)
    place = (c * 4 + x) * 4
    parts[place + y] = mine.astype(BF16)
    own = parts.at[place + y]
    for d in (2, 1, 3):
        push(own, own, S_GY + d, R_GY + 4 - d, at_y(d))
    for d in range(1, 4):
        arrived(own, R_GY + d)
    own = parts.at[pl.ds(place, 4)]
    for d in (2, 1, 3):
        push(own, own, S_GX + d, R_GX + 4 - d, at_x(d))
    for d in range(1, 4):
        arrived(own, R_GX + d)
    own = parts.at[pl.ds(c * 16, 16)]
    push(own, own, S_GC, R_GC, partner)
    arrived(own, R_GC)
    for k in range(32):
        fin[k * piece : (k + 1) * piece, :] = parts[k].astype(F32)

    for n in range(15):
        sent(qg.at[0], S_GATHER + n)
    for n in range(1, 16):
        sent(meta.at[0], S_META + n)
        sent(st_send, S_STATS + n)
    for n in range(1, 32):
        sent(h_recv.at[pl.ds(0, 1)], S_HARD + n)
    for n in range(1, 8):
        sent(hz_recv.at[pl.ds(0, 1)], S_HZ + n)
    for n in range(8):
        sent(qgt.at[0], S_QC + n)
        if n % 4 != 3:
            sent(cs.at[0], S_QX + n)
    sent(zs, S_QZ)
    sent(ac_recv, S_AC)
    for d in range(1, 4):
        sent(ax_recv.at[0], S_AX + d)
        sent(ay_recv.at[0], S_AY + d)
        sent(parts.at[0], S_GY + d)
        sent(parts.at[pl.ds(0, 4)], S_GX + d)
    for d in range(1, 8):
        sent(h_y, S_AZ + d)
    sent(parts.at[pl.ds(0, 16)], S_GC)


def hidden_grads(
    losses, total, qb, pb, projection, losses_out, proj_out, gq_out, gp_hbm, gp, sem
):
    rows = gp.shape[0] // OUT_CHUNKS

    def unload(k):
        at = pl.ds(k * rows, rows)
        return pltpu.make_async_copy(gp.at[at], gp_hbm.at[at], sem.at[k])

    for k in range(OUT_CHUNKS):
        at = pl.ds(k * rows, rows)
        gp[at, :] = contract_last(pb[at, :], projection[...]).astype(BF16)
        unload(k).start()
    gq_out[...] = contract_last(qb[...], projection[...]).astype(BF16)
    proj_out[...] = total[...]
    for k in range(losses_out.shape[0]):
        losses_out[k] = losses[k, 0]
    for k in range(OUT_CHUNKS):
        unload(k).wait()


def local(query_hidden, passage_hidden, projection, positive, hard_ids, passage_len):
    queries, query_len, width = query_hidden.shape
    passages, slots, _ = passage_hidden.shape
    dim = projection.shape[1]
    q_rows, p_rows = queries * query_len, passages * slots
    half = width // 2
    quarter = half // 4
    piece = quarter // 4
    vmem = pl.BlockSpec(memory_space=pltpu.VMEM)
    smem = pl.BlockSpec(memory_space=pltpu.SMEM)
    hbm = pl.BlockSpec(memory_space=pl.ANY)
    scratch = [
        pltpu.VMEM((p_rows, width), BF16),
        pltpu.VMEM((q_rows, dim), F32),
        pltpu.VMEM((p_rows, dim), F32),
        pltpu.VMEM((p_rows, dim), BF16),
        pltpu.VMEM((dim, p_rows), BF16),
        pltpu.VMEM((width, q_rows), BF16),
        pltpu.VMEM((16, q_rows, dim), BF16),
        pltpu.VMEM((16, p_rows, q_rows), BF16),
        pltpu.VMEM((16, passages, q_rows), F32),
        pltpu.VMEM((16, passages, q_rows), F32),
        pltpu.VMEM((p_rows, dim), F32),
        pltpu.VMEM((16, 8, 128), F32),
        pltpu.VMEM((128, 128), F32),
        pltpu.VMEM((passages, 128), F32),
        pltpu.VMEM((passages, 128), F32),
        pltpu.VMEM((passages, 128), F32),
        pltpu.VMEM((8, 128), F32),
        pltpu.VMEM((16, 8, 128), F32),
        pltpu.VMEM((32, 128), F32),
        pltpu.VMEM((8, 128), F32),
        pltpu.VMEM((16, dim, q_rows), BF16),
        pltpu.VMEM((8, dim, q_rows), BF16),
        pltpu.VMEM((8, dim, q_rows), BF16),
        pltpu.VMEM((2, dim, q_rows), F32),
        pltpu.VMEM((8, dim, q_rows), BF16),
        pltpu.VMEM((dim, q_rows), BF16),
        pltpu.VMEM((dim, q_rows), BF16),
        pltpu.VMEM((dim, p_rows), BF16),
        pltpu.VMEM((width, dim), F32),
        pltpu.VMEM((width, dim), BF16),
        pltpu.VMEM((half, dim), BF16),
        pltpu.VMEM((half, dim), BF16),
        pltpu.VMEM((4, quarter, dim), BF16),
        pltpu.VMEM((quarter, dim), F32),
        pltpu.VMEM((4, piece, dim), F32),
        pltpu.VMEM((piece, dim), BF16),
        pltpu.VMEM((8, piece, dim), BF16),
        pltpu.VMEM((32, piece, dim), BF16),
        pltpu.SemaphoreType.DMA((SEND.total,)),
        pltpu.SemaphoreType.DMA((RECV.total,)),
        pltpu.SemaphoreType.DMA((LOCAL.total,)),
    ]
    losses, grad_proj, query_back, passage_back = pl.pallas_call(
        kernel,
        out_shape=(
            jax.ShapeDtypeStruct((8, 128), F32),
            jax.ShapeDtypeStruct((width, dim), F32),
            jax.ShapeDtypeStruct((q_rows, dim), BF16),
            jax.ShapeDtypeStruct((p_rows, dim), BF16),
        ),
        in_specs=[smem, smem, vmem, hbm, vmem, vmem],
        out_specs=(vmem, vmem, vmem, vmem),
        scratch_shapes=scratch,
        compiler_params=pltpu.CompilerParams(
            collective_id=0, has_side_effects=True, vmem_limit_bytes=60 << 20
        ),
        name="late_interaction_step",
    )(
        passage_len,
        positive,
        query_hidden.reshape(q_rows, width),
        passage_hidden.reshape(p_rows, width),
        projection,
        hard_ids,
    )
    losses, grad_proj, grad_query, grad_passage = pl.pallas_call(
        hidden_grads,
        out_shape=(
            jax.ShapeDtypeStruct((queries,), F32),
            jax.ShapeDtypeStruct((width, dim), F32),
            jax.ShapeDtypeStruct((q_rows, width), BF16),
            jax.ShapeDtypeStruct((p_rows, width), BF16),
        ),
        in_specs=[smem, vmem, vmem, vmem, vmem],
        out_specs=(smem, vmem, vmem, hbm),
        scratch_shapes=[
            pltpu.VMEM((p_rows, width), BF16),
            pltpu.SemaphoreType.DMA((OUT_CHUNKS,)),
        ],
        compiler_params=pltpu.CompilerParams(vmem_limit_bytes=16 << 20),
        name="hidden_grads",
    )(losses, grad_proj, query_back, passage_back, projection)
    return (
        losses,
        grad_proj,
        grad_query.reshape(query_hidden.shape),
        grad_passage.reshape(passage_hidden.shape),
    )


def solution(mesh):
    split = Mesh(mesh.devices.reshape(2, 4, 2, 4, 4), AXES)
    placed = (
        P(SPLIT, None, None),
        P(SPLIT, None, None),
        P(),
        P(SPLIT),
        P(SPLIT, None),
        P(SPLIT),
    )
    return jax.shard_map(
        local,
        mesh=split,
        in_specs=placed,
        out_specs=(P(SPLIT), P(), P(SPLIT, None, None), P(SPLIT, None, None)),
        check_vma=False,
    )
```

```python
import functools

import jax
import jax.numpy as jnp
from jax import lax
from jax.experimental import pallas as pl
from jax.experimental.pallas import tpu as pltpu
from jax.sharding import Mesh
from jax.sharding import PartitionSpec as P

MESH = pl.DeviceIdType.MESH
F32 = jnp.float32
BF16 = jnp.bfloat16

AXES = ("zh", "x", "c", "zl", "y")
SPLIT = ("zl", "y", "zh", "x", "c")
norm_eps = 1e-06
EXP2_SCALE = 14.426950408889634
SHIFT = 12.0
HIGHEST = lax.Precision.HIGHEST

GROUP_RELATIVE = [(dz, dx, dc) for dz in range(2) for dx in range(4) for dc in range(2)]

PLANE_RELATIVE = [(dx, dc, dy) for dx in range(4) for dc in range(2) for dy in range(4)]

PLANE_FAR_FIRST = sorted(
    PLANE_RELATIVE[1:], key=lambda r: (-min(r[0], 4 - r[0]) - min(r[2], 4 - r[2]), r)
)


def slot_of(dz, dx, dc):
    return dz * 8 + dx * 2 + dc


def back(d, n):
    return (n - d) % n


def contract_last(left, right):
    return lax.dot_general(
        left, right, (((1,), (1,)), ((), ())), preferred_element_type=F32
    )


def norm_vjp(pre, grad):
    scale = lax.rsqrt(jnp.sum(pre * pre, axis=-1, keepdims=True) + norm_eps)
    along = jnp.sum(pre * grad, axis=-1, keepdims=True)
    return scale * grad - pre * (scale * scale * scale * along)


class Sems:
    def __init__(self):
        self.total = 0

    def take(self, count):
        first = self.total
        self.total += count
        return first


SEND = Sems()
RECV = Sems()
LOCAL = Sems()
S_GATHER, R_GATHER = SEND.take(15), RECV.take(16)
S_META, R_META = SEND.take(16), RECV.take(16)
S_STATS, R_STATS = SEND.take(16), RECV.take(16)
S_HARD, R_HARD = SEND.take(32), RECV.take(32)
S_HZ, R_HZ = SEND.take(8), RECV.take(8)
S_QC, R_QC = SEND.take(8), RECV.take(8)
S_QX, R_QX = SEND.take(8), RECV.take(8)
S_QZ, R_QZ = SEND.take(1), RECV.take(1)
S_RP, R_RP = SEND.take(32), RECV.take(32)
S_AZ, R_AZ = SEND.take(8), RECV.take(8)
S_GP, R_GP = SEND.take(32), RECV.take(32)
P_CHUNKS = 4
OUT_CHUNKS = 8
L_IN = LOCAL.take(P_CHUNKS)
L_QUERY, L_PROJ, L_TOTAL = LOCAL.take(1), LOCAL.take(1), LOCAL.take(1)
L_QB, L_PB = LOCAL.take(1), LOCAL.take(P_CHUNKS)


def kernel(
    plen,
    positive,
    query_hbm,
    passage_hbm,
    projection_hbm,
    hard_ids,
    losses_out,
    total_hbm,
    qb_hbm,
    pb_hbm,
    query_hidden,
    projection,
    ph,
    q_pre,
    p_pre,
    pe,
    pe_t,
    qh_t,
    qg,
    e_ref,
    sums,
    spread_from,
    w_ref,
    pg,
    meta,
    meta_rows,
    counts_ref,
    chosen_ref,
    score_ref,
    st_send,
    st_recv,
    h_recv,
    hz_recv,
    qgt,
    rc,
    cs,
    own_c,
    rx,
    zs,
    rz,
    pb_ref,
    pb_t,
    qb_ref,
    w_loc,
    w_send,
    rp_recv,
    h_send,
    az_recv,
    parts,
    ssem,
    rsem,
    lsem,
):
    zh, x, c = lax.axis_index("zh"), lax.axis_index("x"), lax.axis_index("c")
    zl, y = lax.axis_index("zl"), lax.axis_index("y")
    z = zh * 4 + zl

    def at_x(d):
        return {"x": lax.rem(x + d, 4)}

    def at_y(d):
        return {"y": lax.rem(y + d, 4)}

    def at_z(d):
        there = lax.rem(z + d, 8)
        return {"zh": there // 4, "zl": lax.rem(there, 4)}

    def in_group(dz, dx, dc):
        return {"zh": lax.rem(zh + dz, 2), "x": lax.rem(x + dx, 4), "c": lax.rem(c + dc, 2)}

    def in_plane(dx, dc, dy):
        return {"x": lax.rem(x + dx, 4), "c": lax.rem(c + dc, 2), "y": lax.rem(y + dy, 4)}

    partner = {"c": 1 - c}
    across = {"zh": 1 - zh}

    def group_of(dz, dx, dc):
        return (lax.rem(zh + dz, 2) * 4 + lax.rem(x + dx, 4)) * 2 + lax.rem(c + dc, 2)

    def push(src, dst, s, r, device):
        pltpu.make_async_remote_copy(
            src_ref=src,
            dst_ref=dst,
            send_sem=ssem.at[s],
            recv_sem=rsem.at[r],
            device_id=device,
            device_id_type=MESH,
        ).start()

    def arrived(dst, r):
        pltpu.make_async_remote_copy(
            src_ref=dst,
            dst_ref=dst,
            send_sem=ssem.at[0],
            recv_sem=rsem.at[r],
            device_id=partner,
            device_id_type=MESH,
        ).wait_recv()

    def sent(src, s):
        pltpu.make_async_remote_copy(
            src_ref=src,
            dst_ref=src,
            send_sem=ssem.at[s],
            recv_sem=rsem.at[0],
            device_id=partner,
            device_id_type=MESH,
        ).wait_send()

    rows_in = ph.shape[0] // P_CHUNKS

    def load(k):
        at = pl.ds(k * rows_in, rows_in)
        return pltpu.make_async_copy(passage_hbm.at[at], ph.at[at], lsem.at[L_IN + k])

    load_query = pltpu.make_async_copy(query_hbm, query_hidden, lsem.at[L_QUERY])
    load_proj = pltpu.make_async_copy(projection_hbm, projection, lsem.at[L_PROJ])
    load_query.start()
    load_proj.start()
    for k in range(P_CHUNKS):
        load(k).start()

    barrier = pltpu.get_barrier_semaphore()
    peers = [in_group(*r) for r in GROUP_RELATIVE[1:]]
    peers += [in_plane(*r) for r in PLANE_RELATIVE[1:] if r[2]]
    peers += [at_z(d) for d in range(1, 8) if d != 4]
    for peer in peers:
        pl.semaphore_signal(barrier, inc=1, device_id=peer, device_id_type=MESH)

    load_query.wait()
    load_proj.wait()
    pre = jnp.dot(query_hidden[...], projection[...], preferred_element_type=F32)
    q_pre[...] = pre
    scale = lax.rsqrt(jnp.sum(pre * pre, axis=-1, keepdims=True) + norm_eps)
    qg[0] = (pre * scale).astype(BF16)

    lanes = lax.broadcasted_iota(jnp.int32, (8, 128), 1)
    rows = lax.broadcasted_iota(jnp.int32, (8, 128), 0)
    chosen_row = jnp.zeros((8, 128), F32)
    for k in range(8):
        chosen_row = jnp.where(rows == k, positive[k].astype(F32), chosen_row)
    meta[0] = jnp.where(lanes == 32, chosen_row, 0.0)
    meta[0, :, 0:32] = hard_ids[...].astype(F32)

    pl.semaphore_wait(barrier, len(peers))

    push(qg.at[0], qg.at[slot_of(1, 0, 0)], S_GATHER, R_GATHER + slot_of(1, 0, 0), across)
    for n, d in enumerate((2, 1, 3)):
        to = slot_of(0, back(d, 4), 0)
        push(qg.at[0], qg.at[to], S_GATHER + 1 + n, R_GATHER + to, at_x(d))
    push(qg.at[0], qg.at[1], S_GATHER + 4, R_GATHER + 1, partner)
    for dz, dx, dc in GROUP_RELATIVE[1:]:
        to = slot_of(dz, back(dx, 4), dc)
        push(
            meta.at[0],
            meta.at[to],
            S_META + slot_of(dz, dx, dc),
            R_META + to,
            in_group(dz, dx, dc),
        )

    for k in range(P_CHUNKS):
        load(k).wait()
        at = pl.ds(k * rows_in, rows_in)
        pre = jnp.dot(ph[at, :], projection[...], preferred_element_type=F32)
        p_pre[at, :] = pre
        scale = lax.rsqrt(jnp.sum(pre * pre, axis=-1, keepdims=True) + norm_eps)
        unit = (pre * scale).astype(BF16)
        pe[at, :] = unit
        pe_t[:, at] = unit.T
    qh_t[...] = query_hidden[...].T

    def relay_x(dz, first):
        for n, d in enumerate((1, 2, 3)):
            here, there = slot_of(dz, d, 0), slot_of(dz, d, 1)
            arrived(qg.at[here], R_GATHER + here)
            push(qg.at[here], qg.at[there], first + n, R_GATHER + there, partner)

    def relay_z():
        here = slot_of(1, 0, 0)
        arrived(qg.at[here], R_GATHER + here)
        for n, d in enumerate((2, 1, 3)):
            to = slot_of(1, back(d, 4), 0)
            push(qg.at[here], qg.at[to], S_GATHER + 8 + n, R_GATHER + to, at_x(d))
        push(qg.at[here], qg.at[here + 1], S_GATHER + 11, R_GATHER + here + 1, partner)

    def count_hard():
        for dz, dx, dc in GROUP_RELATIVE:
            slot = slot_of(dz, dx, dc)
            if slot:
                arrived(meta.at[slot], R_META + slot)
            first = pl.multiple_of(group_of(dz, dx, dc) * 8, 8)
            meta_rows[pl.ds(first, 8), :] = meta[slot]
        turned = meta_rows[...].T
        own = (
            group_of(0, 0, 0) * 16 + lax.broadcasted_iota(jnp.int32, (16, 128), 0)
        ).astype(F32)
        counts = jnp.zeros((16, 128), F32)
        for k in range(32):
            counts += (turned[k : k + 1, :] == own).astype(F32)
        counts_ref[...] = counts
        chosen_ref[...] = (turned[32:33, :] == own).astype(F32)

    passages = sums.shape[1]
    step = 4
    height = step * 128

    def grow(k):
        block = qg[k]
        for n in range(passages // step):
            similar = contract_last(pe[n * height : (n + 1) * height, :], block)
            grown = jnp.exp2(similar * EXP2_SCALE)
            for i in range(step):
                p = n * step + i
                token = lax.broadcasted_iota(jnp.int32, (128, grown.shape[1]), 0)
                live = jnp.where(token < plen[p], grown[i * 128 : (i + 1) * 128], 0.0)
                e_ref[k, p * 128 : (p + 1) * 128, :] = live.astype(BF16)
                sums[k, p : p + 1, :] = jnp.sum(live, axis=0, keepdims=True)

    tokens = sums.shape[2]
    spread_from[...] = (
        lax.broadcasted_iota(jnp.int32, (tokens, 128), 0) // 32
        == lax.rem(lax.broadcasted_iota(jnp.int32, (tokens, 128), 1), 8)
    ).astype(F32)
    lane_group = lax.broadcasted_iota(jnp.int32, (passages, 128), 1) // 8

    def score(t):
        pair = sums[pl.ds(2 * t, 2)].reshape(2 * passages, tokens)
        part = jnp.dot(
            0.1 * jnp.log(pair),
            spread_from[...],
            precision=HIGHEST,
            preferred_element_type=F32,
        )
        first = group_of(t // 4, lax.rem(t, 4), 0)
        second = group_of(t // 4, lax.rem(t, 4), 1)
        score_ref[...] += jnp.where(lane_group == first, part[:passages], 0.0) + jnp.where(
            lane_group == second, part[passages:], 0.0
        )

    score_ref[...] = jnp.zeros_like(score_ref)
    grow(0)
    relay_x(0, S_GATHER + 5)
    arrived(qg.at[1], R_GATHER + 1)
    grow(1)

    def forward(t, carry):
        @pl.when(t == 2)
        def _():
            relay_z()

        @pl.when(t == 3)
        def _():
            count_hard()

        @pl.when(t == 5)
        def _():
            relay_x(1, S_GATHER + 12)

        arrived(qg.at[2 * t + 1], R_GATHER + 2 * t + 1)
        score(t - 1)
        grow(2 * t)
        grow(2 * t + 1)
        return carry

    lax.fori_loop(1, 8, forward, 0)

    score(7)
    scores = score_ref[...]
    spread_to = (
        lax.broadcasted_iota(jnp.int32, (128, tokens), 1) // 32
        == lax.rem(lax.broadcasted_iota(jnp.int32, (128, tokens), 0), 8)
    ).astype(F32)
    counts, chosen = counts_ref[...], chosen_ref[...]
    grown = jnp.exp(scores - SHIFT)
    hard = counts * grown
    other_hard = jnp.where(chosen > 0.5, 0.0, hard)
    st_send[...] = jnp.zeros_like(st_send)
    st_send[0:1, :] = jnp.sum(grown, axis=0, keepdims=True)
    st_send[1:2, :] = jnp.sum(other_hard * grown, axis=0, keepdims=True)
    st_send[2:3, :] = jnp.sum(chosen * scores, axis=0, keepdims=True)
    h_recv[0:1, :] = jnp.sum(hard, axis=0, keepdims=True)
    own = h_recv.at[pl.ds(0, 1)]
    for dx, dc, dy in PLANE_FAR_FIRST:
        at = dx * 8 + dc * 4 + dy
        to = back(dx, 4) * 8 + dc * 4 + back(dy, 4)
        push(own, h_recv.at[pl.ds(to, 1)], S_HARD + at, R_HARD + to, in_plane(dx, dc, dy))
    for dz, dx, dc in GROUP_RELATIVE[1:]:
        to = slot_of(dz, back(dx, 4), dc)
        push(
            st_send,
            st_recv.at[to],
            S_STATS + slot_of(dz, dx, dc),
            R_STATS + to,
            in_group(dz, dx, dc),
        )
    w_ref[...] = 1.0 / sums[...]
    pg[...] = jnp.zeros_like(pg)
    for n in range(1, 32):
        arrived(h_recv.at[pl.ds(n, 1)], R_HARD + n)
    hz_recv[0:1, :] = jnp.sum(h_recv[...], axis=0, keepdims=True)
    own = hz_recv.at[pl.ds(0, 1)]
    for d in (4, 3, 5, 2, 6, 1, 7):
        push(own, hz_recv.at[pl.ds(8 - d, 1)], S_HZ + d, R_HZ + 8 - d, at_z(d))
    stats = st_send[...]
    for slot in range(1, 16):
        arrived(st_recv.at[slot], R_STATS + slot)
        stats += st_recv[slot]
    for n in range(1, 8):
        arrived(hz_recv.at[pl.ds(n, 1)], R_HZ + n)
    total = jnp.sum(hz_recv[...], axis=0, keepdims=True)
    boost = (8.0 * 65536.0) / jnp.sum(total, axis=1, keepdims=True)
    partition = stats[0:1, :] + boost * stats[1:2, :]
    loss = jnp.log(partition) + SHIFT - stats[2:3, :]
    own_lane = lanes == group_of(0, 0, 0) * 8 + rows
    losses_out[...] = jnp.broadcast_to(
        jnp.sum(jnp.where(own_lane, loss, 0.0), axis=1, keepdims=True), (8, 128)
    )
    score_grad = grown * (1.0 + boost * other_hard) / partition - chosen

    picked = [
        jnp.where(lane_group == group_of(dz, dx, dc), score_grad, 0.0)
        for dz, dx, dc in GROUP_RELATIVE
    ]
    spread = jnp.dot(
        jnp.concatenate(picked, axis=0),
        spread_to,
        precision=HIGHEST,
        preferred_element_type=F32,
    )
    w_ref[...] *= spread.reshape(w_ref.shape)

    def combine(j):
        arrived(rc.at[j], R_QC + j)
        both = qgt[2 * j + 1].astype(F32) + rc[j].astype(F32)
        side = j // 4
        d = lax.rem(j + 1, 4)

        @pl.when(d != 0)
        def _():
            cs[j] = both.astype(BF16)
            to = side * 4 + (4 - d)
            push(cs.at[j], rx.at[to], S_QX + j, R_QX + to, {"x": lax.rem(x + d, 4)})

        @pl.when(d == 0)
        def _():
            own_c[side] = both

    def over_x(side):
        whole = own_c[side]
        for d in range(1, 4):
            arrived(rx.at[side * 4 + d], R_QX + side * 4 + d)
            whole += rx[side * 4 + d].astype(F32)
        return whole

    def backward(it, carry):
        j = it // 2
        dz = 1 - j // 4
        dx = lax.rem(j + 1, 4)
        dc = 1 - lax.rem(it, 2)
        k = dz * 8 + dx * 2 + dc
        block = qg[k]
        acc = None
        for n in range(passages // step):
            parts = []
            for i in range(step):
                p = n * step + i
                weight = w_ref[k, p : p + 1, :]
                kept = e_ref[k, p * 128 : (p + 1) * 128, :].astype(F32)
                parts.append((kept * weight).astype(BF16))
            coefficient = jnp.concatenate(parts, axis=0)
            at = slice(n * height, (n + 1) * height)
            pg[at, :] += jnp.dot(coefficient, block, preferred_element_type=F32)
            term = jnp.dot(pe_t[:, at], coefficient, preferred_element_type=F32)
            acc = term if acc is None else acc + term
        qgt[it] = acc.astype(BF16)

        @pl.when(dc == 1)
        def _():
            push(qgt.at[it], rc.at[j], S_QC + j, R_QC + j, partner)

            @pl.when(it >= 2)
            def _():
                combine(j - 1)

        @pl.when(it == 13)
        def _():
            zs[...] = over_x(0).astype(BF16)
            push(zs, rz, S_QZ, R_QZ, across)

        return carry

    lax.fori_loop(0, 16, backward, 0)
    combine(7)

    def store_pb(k):
        at = pl.ds(k * rows_in, rows_in)
        return pltpu.make_async_copy(pb_ref.at[at], pb_hbm.at[at], lsem.at[L_PB + k])

    store_qb = pltpu.make_async_copy(qb_ref, qb_hbm, lsem.at[L_QB])
    store_total = pltpu.make_async_copy(parts, total_hbm, lsem.at[L_TOTAL])

    for k in range(P_CHUNKS):
        at = pl.ds(k * rows_in, rows_in)
        pb = norm_vjp(p_pre[at, :], pg[at, :]).astype(BF16)
        pb_t[:, at] = pb.T
        pb_ref[at, :] = pb
        store_pb(k).start()
    w_t = jnp.dot(pb_t[...], ph[...], preferred_element_type=F32)
    w_loc[...] = w_t.T

    arrived(rz, R_QZ)
    whole = over_x(1) + rz[...].astype(F32)
    qb = norm_vjp(q_pre[...], whole.T).astype(BF16)
    qb_ref[...] = qb
    whole = w_loc[...] + jnp.dot(qh_t[...], qb, preferred_element_type=F32)
    w_loc[...] = whole

    piece = h_send.shape[0]
    for k in range(32):
        w_send[k] = whole[k * piece : (k + 1) * piece].astype(BF16)
    here = (c * 4 + x) * 4 + y
    for dx, dc, dy in PLANE_FAR_FIRST:
        at = dx * 8 + dc * 4 + dy
        to = back(dx, 4) * 8 + dc * 4 + back(dy, 4)
        there = (lax.rem(c + dc, 2) * 4 + lax.rem(x + dx, 4)) * 4 + lax.rem(y + dy, 4)
        push(w_send.at[there], rp_recv.at[to], S_RP + at, R_RP + to, in_plane(dx, dc, dy))
    store_qb.start()
    mine = w_loc[pl.ds(pl.multiple_of(here * piece, 8), piece), :]
    for n in range(1, 32):
        arrived(rp_recv.at[n], R_RP + n)
        mine += rp_recv[n].astype(F32)
    h_send[...] = mine.astype(BF16)
    for d in (4, 3, 5, 2, 6, 1, 7):
        push(h_send, az_recv.at[z], S_AZ + d, R_AZ + 8 - d, at_z(d))
    az_recv[z] = h_send[...]
    for d in range(1, 8):
        arrived(az_recv.at[0], R_AZ + d)
    mine = az_recv[0].astype(F32)
    for k in range(1, 8):
        mine += az_recv[k].astype(F32)
    parts[here] = mine.astype(BF16)
    for dx, dc, dy in PLANE_FAR_FIRST:
        at = dx * 8 + dc * 4 + dy
        to = back(dx, 4) * 8 + dc * 4 + back(dy, 4)
        push(parts.at[here], parts.at[here], S_GP + at, R_GP + to, in_plane(dx, dc, dy))
    for n in range(1, 32):
        arrived(parts.at[0], R_GP + n)
    store_total.start()

    for n in range(15):
        sent(qg.at[0], S_GATHER + n)
    for n in range(1, 16):
        sent(meta.at[0], S_META + n)
        sent(st_send, S_STATS + n)
    for n in range(1, 32):
        sent(h_recv.at[pl.ds(0, 1)], S_HARD + n)
    for n in range(1, 8):
        sent(hz_recv.at[pl.ds(0, 1)], S_HZ + n)
    for n in range(8):
        sent(qgt.at[0], S_QC + n)
        if n % 4 != 3:
            sent(cs.at[0], S_QX + n)
    sent(zs, S_QZ)
    for n in range(1, 32):
        sent(w_send.at[0], S_RP + n)
        sent(parts.at[0], S_GP + n)
    for d in range(1, 8):
        sent(h_send, S_AZ + d)
    store_qb.wait()
    for k in range(P_CHUNKS):
        store_pb(k).wait()
    store_total.wait()


def hidden_grads(
    losses_hbm,
    total_hbm,
    qb_hbm,
    pb_hbm,
    projection_hbm,
    losses_out,
    proj_hbm,
    gq_hbm,
    gp_hbm,
    losses,
    total,
    qb,
    pb,
    projection,
    proj,
    gq,
    gp,
    sem,
):
    rows = gp.shape[0] // OUT_CHUNKS
    loads = [
        pltpu.make_async_copy(src, dst, sem.at[n])
        for n, (src, dst) in enumerate(
            (
                (projection_hbm, projection),
                (pb_hbm, pb),
                (qb_hbm, qb),
                (total_hbm, total),
                (losses_hbm, losses),
            )
        )
    ]

    def unload(k):
        at = pl.ds(k * rows, rows)
        return pltpu.make_async_copy(gp.at[at], gp_hbm.at[at], sem.at[5 + k])

    store_proj = pltpu.make_async_copy(proj, proj_hbm, sem.at[5 + OUT_CHUNKS])
    store_gq = pltpu.make_async_copy(gq, gq_hbm, sem.at[6 + OUT_CHUNKS])
    for copy in loads:
        copy.start()
    loads[0].wait()
    loads[1].wait()
    for k in range(OUT_CHUNKS):
        at = pl.ds(k * rows, rows)
        gp[at, :] = contract_last(pb[at, :], projection[...]).astype(BF16)
        unload(k).start()
    loads[2].wait()
    gq[...] = contract_last(qb[...], projection[...]).astype(BF16)
    store_gq.start()
    loads[3].wait()
    piece = total.shape[1]
    for k in range(total.shape[0]):
        proj[k * piece : (k + 1) * piece, :] = total[k].astype(F32)
    store_proj.start()
    loads[4].wait()
    for k in range(losses_out.shape[0]):
        losses_out[k] = losses[k, 0]
    for k in range(OUT_CHUNKS):
        unload(k).wait()
    store_gq.wait()
    store_proj.wait()


def local(query_hidden, passage_hidden, projection, positive, hard_ids, passage_len):
    queries, query_len, width = query_hidden.shape
    passages, slots, _ = passage_hidden.shape
    dim = projection.shape[1]
    q_rows, p_rows = queries * query_len, passages * slots
    piece = width // 32
    vmem = pl.BlockSpec(memory_space=pltpu.VMEM)
    smem = pl.BlockSpec(memory_space=pltpu.SMEM)
    hbm = pl.BlockSpec(memory_space=pl.ANY)
    scratch = [
        pltpu.VMEM((q_rows, width), BF16),
        pltpu.VMEM((width, dim), BF16),
        pltpu.VMEM((p_rows, width), BF16),
        pltpu.VMEM((q_rows, dim), F32),
        pltpu.VMEM((p_rows, dim), F32),
        pltpu.VMEM((p_rows, dim), BF16),
        pltpu.VMEM((dim, p_rows), BF16),
        pltpu.VMEM((width, q_rows), BF16),
        pltpu.VMEM((16, q_rows, dim), BF16),
        pltpu.VMEM((16, p_rows, q_rows), BF16),
        pltpu.VMEM((16, passages, q_rows), F32),
        pltpu.VMEM((q_rows, 128), F32),
        pltpu.VMEM((16, passages, q_rows), F32),
        pltpu.VMEM((p_rows, dim), F32),
        pltpu.VMEM((16, 8, 128), F32),
        pltpu.VMEM((128, 128), F32),
        pltpu.VMEM((passages, 128), F32),
        pltpu.VMEM((passages, 128), F32),
        pltpu.VMEM((passages, 128), F32),
        pltpu.VMEM((8, 128), F32),
        pltpu.VMEM((16, 8, 128), F32),
        pltpu.VMEM((32, 128), F32),
        pltpu.VMEM((8, 128), F32),
        pltpu.VMEM((16, dim, q_rows), BF16),
        pltpu.VMEM((8, dim, q_rows), BF16),
        pltpu.VMEM((8, dim, q_rows), BF16),
        pltpu.VMEM((2, dim, q_rows), F32),
        pltpu.VMEM((8, dim, q_rows), BF16),
        pltpu.VMEM((dim, q_rows), BF16),
        pltpu.VMEM((dim, q_rows), BF16),
        pltpu.VMEM((p_rows, dim), BF16),
        pltpu.VMEM((dim, p_rows), BF16),
        pltpu.VMEM((q_rows, dim), BF16),
        pltpu.VMEM((width, dim), F32),
        pltpu.VMEM((32, piece, dim), BF16),
        pltpu.VMEM((32, piece, dim), BF16),
        pltpu.VMEM((piece, dim), BF16),
        pltpu.VMEM((8, piece, dim), BF16),
        pltpu.VMEM((32, piece, dim), BF16),
        pltpu.SemaphoreType.DMA((SEND.total,)),
        pltpu.SemaphoreType.DMA((RECV.total,)),
        pltpu.SemaphoreType.DMA((LOCAL.total,)),
    ]
    losses, total, query_back, passage_back = pl.pallas_call(
        kernel,
        out_shape=(
            jax.ShapeDtypeStruct((8, 128), F32),
            jax.ShapeDtypeStruct((32, piece, dim), BF16),
            jax.ShapeDtypeStruct((q_rows, dim), BF16),
            jax.ShapeDtypeStruct((p_rows, dim), BF16),
        ),
        in_specs=[smem, smem, hbm, hbm, hbm, vmem],
        out_specs=(vmem, hbm, hbm, hbm),
        scratch_shapes=scratch,
        compiler_params=pltpu.CompilerParams(
            collective_id=0, has_side_effects=True, vmem_limit_bytes=60 << 20
        ),
        name="late_interaction_step",
    )(
        passage_len,
        positive,
        query_hidden.reshape(q_rows, width),
        passage_hidden.reshape(p_rows, width),
        projection,
        hard_ids,
    )
    losses, grad_proj, grad_query, grad_passage = pl.pallas_call(
        hidden_grads,
        out_shape=(
            jax.ShapeDtypeStruct((queries,), F32),
            jax.ShapeDtypeStruct((width, dim), F32),
            jax.ShapeDtypeStruct((q_rows, width), BF16),
            jax.ShapeDtypeStruct((p_rows, width), BF16),
        ),
        in_specs=[hbm] * 5,
        out_specs=(smem, hbm, hbm, hbm),
        scratch_shapes=[
            pltpu.SMEM((8, 128), F32),
            pltpu.VMEM((32, piece, dim), BF16),
            pltpu.VMEM((q_rows, dim), BF16),
            pltpu.VMEM((p_rows, dim), BF16),
            pltpu.VMEM((width, dim), BF16),
            pltpu.VMEM((width, dim), F32),
            pltpu.VMEM((q_rows, width), BF16),
            pltpu.VMEM((p_rows, width), BF16),
            pltpu.SemaphoreType.DMA((7 + OUT_CHUNKS,)),
        ],
        compiler_params=pltpu.CompilerParams(vmem_limit_bytes=60 << 20),
        name="hidden_grads",
    )(losses, total, query_back, passage_back, projection)
    return (
        losses,
        grad_proj,
        grad_query.reshape(query_hidden.shape),
        grad_passage.reshape(passage_hidden.shape),
    )


def solution(mesh):
    split = Mesh(mesh.devices.reshape(2, 4, 2, 4, 4), AXES)
    placed = (
        P(SPLIT, None, None),
        P(SPLIT, None, None),
        P(),
        P(SPLIT),
        P(SPLIT, None),
        P(SPLIT),
    )
    return jax.shard_map(
        local,
        mesh=split,
        in_specs=placed,
        out_specs=(P(SPLIT), P(), P(SPLIT, None, None), P(SPLIT, None, None)),
        check_vma=False,
    )
```

```python
import functools

import jax
import jax.numpy as jnp
from jax import lax
from jax.experimental import pallas as pl
from jax.experimental.pallas import tpu as pltpu
from jax.sharding import Mesh
from jax.sharding import PartitionSpec as P

MESH = pl.DeviceIdType.MESH
F32 = jnp.float32
BF16 = jnp.bfloat16

AXES = ("zh", "x", "c", "zl", "y")
SPLIT = ("zl", "y", "zh", "x", "c")
norm_eps = 1e-06
EXP2_SCALE = 14.426950408889634
SHIFT = 12.0
HIGHEST = lax.Precision.HIGHEST

GROUP_RELATIVE = [(dz, dx, dc) for dz in range(2) for dx in range(4) for dc in range(2)]

PLANE_RELATIVE = [(dx, dc, dy) for dx in range(4) for dc in range(2) for dy in range(4)]

PLANE_FAR_FIRST = sorted(
    PLANE_RELATIVE[1:], key=lambda r: (-min(r[0], 4 - r[0]) - min(r[2], 4 - r[2]), r)
)


def slot_of(dz, dx, dc):
    return dz * 8 + dx * 2 + dc


def back(d, n):
    return (n - d) % n


def contract_last(left, right):
    return lax.dot_general(
        left, right, (((1,), (1,)), ((), ())), preferred_element_type=F32
    )


def norm_vjp(pre, grad):
    scale = lax.rsqrt(jnp.sum(pre * pre, axis=-1, keepdims=True) + norm_eps)
    along = jnp.sum(pre * grad, axis=-1, keepdims=True)
    return scale * grad - pre * (scale * scale * scale * along)


class Sems:
    def __init__(self):
        self.total = 0

    def take(self, count):
        first = self.total
        self.total += count
        return first


SEND = Sems()
RECV = Sems()
LOCAL = Sems()
S_GATHER, R_GATHER = SEND.take(15), RECV.take(16)
S_META, R_META = SEND.take(16), RECV.take(16)
S_STATS, R_STATS = SEND.take(16), RECV.take(16)
S_HARD, R_HARD = SEND.take(32), RECV.take(32)
S_HZ, R_HZ = SEND.take(8), RECV.take(8)
S_QC, R_QC = SEND.take(8), RECV.take(8)
S_QX, R_QX = SEND.take(8), RECV.take(8)
S_QZ, R_QZ = SEND.take(1), RECV.take(1)
S_RP, R_RP = SEND.take(32), RECV.take(32)
S_AZ, R_AZ = SEND.take(8), RECV.take(8)
S_GP, R_GP = SEND.take(32), RECV.take(32)
P_CHUNKS = 4
FSTEP = 4
BSTEP = 4
OUT_CHUNKS = 8
L_IN = LOCAL.take(P_CHUNKS)
L_QUERY, L_PROJ = LOCAL.take(1), LOCAL.take(1)


def kernel(
    plen,
    positive,
    query_hbm,
    passage_hbm,
    projection_hbm,
    hard_ids,
    losses_out,
    total_out,
    gq_out,
    gp_out,
    query_hidden,
    projection,
    ph,
    q_pre,
    p_pre,
    pe,
    pe_t,
    qh_t,
    qg,
    e_ref,
    sums,
    spread_from,
    one_lane,
    w_ref,
    pg,
    meta,
    meta_rows,
    counts_ref,
    chosen_ref,
    score_ref,
    st_send,
    st_recv,
    h_recv,
    hz_recv,
    qgt,
    rc,
    cs,
    own_c,
    rx,
    zs,
    rz,
    pb_ref,
    pb_t,
    qb_ref,
    w_loc,
    w_send,
    rp_recv,
    h_send,
    az_recv,
    parts,
    ssem,
    rsem,
    lsem,
):
    zh, x, c = lax.axis_index("zh"), lax.axis_index("x"), lax.axis_index("c")
    zl, y = lax.axis_index("zl"), lax.axis_index("y")
    z = zh * 4 + zl

    def at_x(d):
        return {"x": lax.rem(x + d, 4)}

    def at_y(d):
        return {"y": lax.rem(y + d, 4)}

    def at_z(d):
        there = lax.rem(z + d, 8)
        return {"zh": there // 4, "zl": lax.rem(there, 4)}

    def in_group(dz, dx, dc):
        return {"zh": lax.rem(zh + dz, 2), "x": lax.rem(x + dx, 4), "c": lax.rem(c + dc, 2)}

    def in_plane(dx, dc, dy):
        return {"x": lax.rem(x + dx, 4), "c": lax.rem(c + dc, 2), "y": lax.rem(y + dy, 4)}

    partner = {"c": 1 - c}
    across = {"zh": 1 - zh}

    def group_of(dz, dx, dc):
        return (lax.rem(zh + dz, 2) * 4 + lax.rem(x + dx, 4)) * 2 + lax.rem(c + dc, 2)

    def push(src, dst, s, r, device):
        pltpu.make_async_remote_copy(
            src_ref=src,
            dst_ref=dst,
            send_sem=ssem.at[s],
            recv_sem=rsem.at[r],
            device_id=device,
            device_id_type=MESH,
        ).start()

    def arrived(dst, r):
        pltpu.make_async_remote_copy(
            src_ref=dst,
            dst_ref=dst,
            send_sem=ssem.at[0],
            recv_sem=rsem.at[r],
            device_id=partner,
            device_id_type=MESH,
        ).wait_recv()

    def sent(src, s):
        pltpu.make_async_remote_copy(
            src_ref=src,
            dst_ref=src,
            send_sem=ssem.at[s],
            recv_sem=rsem.at[0],
            device_id=partner,
            device_id_type=MESH,
        ).wait_send()

    rows_in = ph.shape[0] // P_CHUNKS

    def load(k):
        at = pl.ds(k * rows_in, rows_in)
        return pltpu.make_async_copy(passage_hbm.at[at], ph.at[at], lsem.at[L_IN + k])

    load_query = pltpu.make_async_copy(query_hbm, query_hidden, lsem.at[L_QUERY])
    load_proj = pltpu.make_async_copy(projection_hbm, projection, lsem.at[L_PROJ])
    load_query.start()
    load_proj.start()
    for k in range(P_CHUNKS):
        load(k).start()

    barrier = pltpu.get_barrier_semaphore()
    peers = [in_group(*r) for r in GROUP_RELATIVE[1:]]
    peers += [in_plane(*r) for r in PLANE_RELATIVE[1:] if r[2]]
    peers += [at_z(d) for d in range(1, 8) if d != 4]
    for peer in peers:
        pl.semaphore_signal(barrier, inc=1, device_id=peer, device_id_type=MESH)

    load_query.wait()
    load_proj.wait()
    pre = jnp.dot(query_hidden[...], projection[...], preferred_element_type=F32)
    q_pre[...] = pre
    scale = lax.rsqrt(jnp.sum(pre * pre, axis=-1, keepdims=True) + norm_eps)
    qg[0] = (pre * scale).astype(BF16)

    lanes = lax.broadcasted_iota(jnp.int32, (8, 128), 1)
    rows = lax.broadcasted_iota(jnp.int32, (8, 128), 0)
    chosen_row = jnp.zeros((8, 128), F32)
    for k in range(8):
        chosen_row = jnp.where(rows == k, positive[k].astype(F32), chosen_row)
    meta[0] = jnp.where(lanes == 32, chosen_row, 0.0)
    meta[0, :, 0:32] = hard_ids[...].astype(F32)

    pl.semaphore_wait(barrier, len(peers))

    push(qg.at[0], qg.at[slot_of(1, 0, 0)], S_GATHER, R_GATHER + slot_of(1, 0, 0), across)
    for n, d in enumerate((2, 1, 3)):
        to = slot_of(0, back(d, 4), 0)
        push(qg.at[0], qg.at[to], S_GATHER + 1 + n, R_GATHER + to, at_x(d))
    push(qg.at[0], qg.at[1], S_GATHER + 4, R_GATHER + 1, partner)
    for dz, dx, dc in GROUP_RELATIVE[1:]:
        to = slot_of(dz, back(dx, 4), dc)
        push(
            meta.at[0],
            meta.at[to],
            S_META + slot_of(dz, dx, dc),
            R_META + to,
            in_group(dz, dx, dc),
        )

    first_lane = lax.broadcasted_iota(jnp.int32, (128, 128), 1) == 0
    token = lax.broadcasted_iota(jnp.int32, (128, 128), 0)
    for p in range(plen.shape[0]):
        padding = first_lane & (token >= plen[p])
        pe[p * 128 : (p + 1) * 128, 128:256] = jnp.where(padding, -100.0, 0.0).astype(BF16)
    one_lane[...] = (lax.broadcasted_iota(jnp.int32, one_lane.shape, 1) == 0).astype(BF16)
    for k in range(P_CHUNKS):
        load(k).wait()
        at = pl.ds(k * rows_in, rows_in)
        pre = jnp.dot(ph[at, :], projection[...], preferred_element_type=F32)
        p_pre[at, :] = pre
        scale = lax.rsqrt(jnp.sum(pre * pre, axis=-1, keepdims=True) + norm_eps)
        unit = (pre * scale).astype(BF16)
        pe[at, 0:128] = unit
        pe_t[:, at] = unit.T
    qh_t[...] = query_hidden[...].T

    def relay_x(dz, first):
        for n, d in enumerate((1, 2, 3)):
            here, there = slot_of(dz, d, 0), slot_of(dz, d, 1)
            arrived(qg.at[here], R_GATHER + here)
            push(qg.at[here], qg.at[there], first + n, R_GATHER + there, partner)

    def relay_z():
        here = slot_of(1, 0, 0)
        arrived(qg.at[here], R_GATHER + here)
        for n, d in enumerate((2, 1, 3)):
            to = slot_of(1, back(d, 4), 0)
            push(qg.at[here], qg.at[to], S_GATHER + 8 + n, R_GATHER + to, at_x(d))
        push(qg.at[here], qg.at[here + 1], S_GATHER + 11, R_GATHER + here + 1, partner)

    def count_hard():
        for dz, dx, dc in GROUP_RELATIVE:
            slot = slot_of(dz, dx, dc)
            if slot:
                arrived(meta.at[slot], R_META + slot)
            first = pl.multiple_of(group_of(dz, dx, dc) * 8, 8)
            meta_rows[pl.ds(first, 8), :] = meta[slot]
        turned = meta_rows[...].T
        own = (
            group_of(0, 0, 0) * 16 + lax.broadcasted_iota(jnp.int32, (16, 128), 0)
        ).astype(F32)
        counts = jnp.zeros((16, 128), F32)
        for k in range(32):
            counts += (turned[k : k + 1, :] == own).astype(F32)
        counts_ref[...] = counts
        chosen_ref[...] = (turned[32:33, :] == own).astype(F32)

    passages = sums.shape[1]
    step = FSTEP
    height = step * 128

    def grow(k):
        block = jnp.concatenate([qg[k], one_lane[...]], axis=1)
        for n in range(passages // step):
            similar = contract_last(pe[n * height : (n + 1) * height, :], block)
            grown = jnp.exp2(similar * EXP2_SCALE)
            for i in range(step):
                p = n * step + i
                live = grown[i * 128 : (i + 1) * 128]
                e_ref[k, p * 128 : (p + 1) * 128, :] = live.astype(BF16)
                sums[k, p : p + 1, :] = jnp.sum(live, axis=0, keepdims=True)

    tokens = sums.shape[2]
    spread_from[...] = (
        lax.broadcasted_iota(jnp.int32, (tokens, 128), 0) // 32
        == lax.rem(lax.broadcasted_iota(jnp.int32, (tokens, 128), 1), 8)
    ).astype(F32)
    lane_group = lax.broadcasted_iota(jnp.int32, (passages, 128), 1) // 8

    def score(t):
        pair = sums[pl.ds(2 * t, 2)].reshape(2 * passages, tokens)
        part = jnp.dot(
            0.1 * jnp.log(pair),
            spread_from[...],
            precision=HIGHEST,
            preferred_element_type=F32,
        )
        first = group_of(t // 4, lax.rem(t, 4), 0)
        second = group_of(t // 4, lax.rem(t, 4), 1)
        score_ref[...] += jnp.where(lane_group == first, part[:passages], 0.0) + jnp.where(
            lane_group == second, part[passages:], 0.0
        )

    score_ref[...] = jnp.zeros_like(score_ref)
    grow(0)
    relay_x(0, S_GATHER + 5)
    arrived(qg.at[1], R_GATHER + 1)
    grow(1)

    def forward(t, carry):
        @pl.when(t == 2)
        def _():
            relay_z()

        @pl.when(t == 3)
        def _():
            count_hard()

        @pl.when(t == 5)
        def _():
            relay_x(1, S_GATHER + 12)

        arrived(qg.at[2 * t + 1], R_GATHER + 2 * t + 1)
        score(t - 1)
        grow(2 * t)
        grow(2 * t + 1)
        return carry

    lax.fori_loop(1, 8, forward, 0)

    score(7)
    scores = score_ref[...]
    spread_to = (
        lax.broadcasted_iota(jnp.int32, (128, tokens), 1) // 32
        == lax.rem(lax.broadcasted_iota(jnp.int32, (128, tokens), 0), 8)
    ).astype(F32)
    counts, chosen = counts_ref[...], chosen_ref[...]
    grown = jnp.exp(scores - SHIFT)
    hard = counts * grown
    other_hard = jnp.where(chosen > 0.5, 0.0, hard)
    st_send[...] = jnp.zeros_like(st_send)
    st_send[0:1, :] = jnp.sum(grown, axis=0, keepdims=True)
    st_send[1:2, :] = jnp.sum(other_hard * grown, axis=0, keepdims=True)
    st_send[2:3, :] = jnp.sum(chosen * scores, axis=0, keepdims=True)
    h_recv[0:1, :] = jnp.sum(hard, axis=0, keepdims=True)
    own = h_recv.at[pl.ds(0, 1)]
    for dx, dc, dy in PLANE_FAR_FIRST:
        at = dx * 8 + dc * 4 + dy
        to = back(dx, 4) * 8 + dc * 4 + back(dy, 4)
        push(own, h_recv.at[pl.ds(to, 1)], S_HARD + at, R_HARD + to, in_plane(dx, dc, dy))
    for dz, dx, dc in GROUP_RELATIVE[1:]:
        to = slot_of(dz, back(dx, 4), dc)
        push(
            st_send,
            st_recv.at[to],
            S_STATS + slot_of(dz, dx, dc),
            R_STATS + to,
            in_group(dz, dx, dc),
        )
    w_ref[...] = 1.0 / sums[...]
    pg[...] = jnp.zeros_like(pg)
    for n in range(1, 32):
        arrived(h_recv.at[pl.ds(n, 1)], R_HARD + n)
    hz_recv[0:1, :] = jnp.sum(h_recv[...], axis=0, keepdims=True)
    own = hz_recv.at[pl.ds(0, 1)]
    for d in (4, 3, 5, 2, 6, 1, 7):
        push(own, hz_recv.at[pl.ds(8 - d, 1)], S_HZ + d, R_HZ + 8 - d, at_z(d))
    stats = st_send[...]
    for slot in range(1, 16):
        arrived(st_recv.at[slot], R_STATS + slot)
        stats += st_recv[slot]
    for n in range(1, 8):
        arrived(hz_recv.at[pl.ds(n, 1)], R_HZ + n)
    total = jnp.sum(hz_recv[...], axis=0, keepdims=True)
    boost = (8.0 * 65536.0) / jnp.sum(total, axis=1, keepdims=True)
    partition = stats[0:1, :] + boost * stats[1:2, :]
    loss = jnp.log(partition) + SHIFT - stats[2:3, :]
    own_lane = lanes == group_of(0, 0, 0) * 8 + rows
    losses_out[...] = jnp.broadcast_to(
        jnp.sum(jnp.where(own_lane, loss, 0.0), axis=1, keepdims=True), (8, 128)
    )
    score_grad = grown * (1.0 + boost * other_hard) / partition - chosen

    picked = [
        jnp.where(lane_group == group_of(dz, dx, dc), score_grad, 0.0)
        for dz, dx, dc in GROUP_RELATIVE
    ]
    spread = jnp.dot(
        jnp.concatenate(picked, axis=0),
        spread_to,
        precision=HIGHEST,
        preferred_element_type=F32,
    )
    w_ref[...] *= spread.reshape(w_ref.shape)

    def combine(j):
        arrived(rc.at[j], R_QC + j)
        both = qgt[2 * j + 1].astype(F32) + rc[j].astype(F32)
        side = j // 4
        d = lax.rem(j + 1, 4)

        @pl.when(d != 0)
        def _():
            cs[j] = both.astype(BF16)
            to = side * 4 + (4 - d)
            push(cs.at[j], rx.at[to], S_QX + j, R_QX + to, {"x": lax.rem(x + d, 4)})

        @pl.when(d == 0)
        def _():
            own_c[side] = both

    def over_x(side):
        whole = own_c[side]
        for d in range(1, 4):
            arrived(rx.at[side * 4 + d], R_QX + side * 4 + d)
            whole += rx[side * 4 + d].astype(F32)
        return whole

    def backward(j, carry):
        dz = 1 - j // 4
        k = dz * 8 + lax.rem(j + 1, 4) * 2
        both = qg[pl.ds(k, 2)].reshape(2 * tokens, qg.shape[2])
        acc = None
        for n in range(passages // BSTEP):
            parts = []
            for i in range(BSTEP):
                p = n * BSTEP + i
                pair = [
                    (
                        e_ref[k + m, p * 128 : (p + 1) * 128, :].astype(F32)
                        * w_ref[k + m, p : p + 1, :]
                    ).astype(BF16)
                    for m in range(2)
                ]
                parts.append(jnp.concatenate(pair, axis=1))
            coefficient = jnp.concatenate(parts, axis=0) if BSTEP > 1 else parts[0]
            at = slice(n * BSTEP * 128, (n + 1) * BSTEP * 128)
            pg[at, :] += jnp.dot(coefficient, both, preferred_element_type=F32)
            term = jnp.dot(pe_t[:, at], coefficient, preferred_element_type=F32)
            acc = term if acc is None else acc + term
        qgt[2 * j] = acc[:, tokens:].astype(BF16)
        push(qgt.at[2 * j], rc.at[j], S_QC + j, R_QC + j, partner)
        qgt[2 * j + 1] = acc[:, :tokens].astype(BF16)

        @pl.when(j >= 1)
        def _():
            combine(j - 1)

        @pl.when(j == 6)
        def _():
            zs[...] = over_x(0).astype(BF16)
            push(zs, rz, S_QZ, R_QZ, across)

        return carry

    lax.fori_loop(0, 8, backward, 0)
    combine(7)

    for k in range(P_CHUNKS):
        at = pl.ds(k * rows_in, rows_in)
        pb = norm_vjp(p_pre[at, :], pg[at, :]).astype(BF16)
        pb_t[:, at] = pb.T
        pb_ref[at, :] = pb
    w_t = jnp.dot(pb_t[...], ph[...], preferred_element_type=F32)
    w_loc[...] = w_t.T

    arrived(rz, R_QZ)
    whole = over_x(1) + rz[...].astype(F32)
    qb = norm_vjp(q_pre[...], whole.T).astype(BF16)
    qb_ref[...] = qb
    whole = w_loc[...] + jnp.dot(qh_t[...], qb, preferred_element_type=F32)
    w_loc[...] = whole

    piece = h_send.shape[0]
    for k in range(32):
        w_send[k] = whole[k * piece : (k + 1) * piece].astype(BF16)
    here = (c * 4 + x) * 4 + y
    for dx, dc, dy in PLANE_FAR_FIRST:
        at = dx * 8 + dc * 4 + dy
        to = back(dx, 4) * 8 + dc * 4 + back(dy, 4)
        there = (lax.rem(c + dc, 2) * 4 + lax.rem(x + dx, 4)) * 4 + lax.rem(y + dy, 4)
        push(w_send.at[there], rp_recv.at[to], S_RP + at, R_RP + to, in_plane(dx, dc, dy))
    gq_out[...] = contract_last(qb_ref[...], projection[...]).astype(BF16)
    for k in range(P_CHUNKS):
        at = pl.ds(k * rows_in, rows_in)
        gp_out[at, :] = contract_last(pb_ref[at, :], projection[...]).astype(BF16)
    mine = w_loc[pl.ds(pl.multiple_of(here * piece, 8), piece), :]
    for n in range(1, 32):
        arrived(rp_recv.at[n], R_RP + n)
        mine += rp_recv[n].astype(F32)
    h_send[...] = mine.astype(BF16)
    for d in (4, 3, 5, 2, 6, 1, 7):
        push(h_send, az_recv.at[z], S_AZ + d, R_AZ + 8 - d, at_z(d))
    az_recv[z] = h_send[...]
    for d in range(1, 8):
        arrived(az_recv.at[0], R_AZ + d)
    mine = az_recv[0].astype(F32)
    for k in range(1, 8):
        mine += az_recv[k].astype(F32)
    parts[here] = mine.astype(BF16)
    for dx, dc, dy in PLANE_FAR_FIRST:
        at = dx * 8 + dc * 4 + dy
        to = back(dx, 4) * 8 + dc * 4 + back(dy, 4)
        push(parts.at[here], parts.at[here], S_GP + at, R_GP + to, in_plane(dx, dc, dy))
    for n in range(1, 32):
        arrived(parts.at[0], R_GP + n)
    piece = total_out.shape[0] // 32
    for k in range(32):
        total_out[k * piece : (k + 1) * piece, :] = parts[k].astype(F32)

    for n in range(15):
        sent(qg.at[0], S_GATHER + n)
    for n in range(1, 16):
        sent(meta.at[0], S_META + n)
        sent(st_send, S_STATS + n)
    for n in range(1, 32):
        sent(h_recv.at[pl.ds(0, 1)], S_HARD + n)
    for n in range(1, 8):
        sent(hz_recv.at[pl.ds(0, 1)], S_HZ + n)
    for n in range(8):
        sent(qgt.at[0], S_QC + n)
        if n % 4 != 3:
            sent(cs.at[0], S_QX + n)
    sent(zs, S_QZ)
    for n in range(1, 32):
        sent(w_send.at[0], S_RP + n)
        sent(parts.at[0], S_GP + n)
    for d in range(1, 8):
        sent(h_send, S_AZ + d)


def write_out(losses, total, gq, gp, losses_out, total_hbm, gq_hbm, gp_hbm, sem):
    rows = gp.shape[0] // OUT_CHUNKS
    copies = []
    for k in range(OUT_CHUNKS):
        at = pl.ds(k * rows, rows)
        copies.append((gp.at[at], gp_hbm.at[at]))
    copies += [(gq, gq_hbm), (total, total_hbm)]
    copies = [pltpu.make_async_copy(a, b, sem.at[n]) for n, (a, b) in enumerate(copies)]
    for copy in copies:
        copy.start()
    for k in range(losses_out.shape[0]):
        losses_out[k] = jnp.sum(losses[k : k + 1, 0:1])
    for copy in copies:
        copy.wait()


def local(query_hidden, passage_hidden, projection, positive, hard_ids, passage_len):
    queries, query_len, width = query_hidden.shape
    passages, slots, _ = passage_hidden.shape
    dim = projection.shape[1]
    q_rows, p_rows = queries * query_len, passages * slots
    piece = width // 32
    vmem = pl.BlockSpec(memory_space=pltpu.VMEM)
    smem = pl.BlockSpec(memory_space=pltpu.SMEM)
    hbm = pl.BlockSpec(memory_space=pl.ANY)
    scratch = [
        pltpu.VMEM((q_rows, width), BF16),
        pltpu.VMEM((width, dim), BF16),
        pltpu.VMEM((p_rows, width), BF16),
        pltpu.VMEM((q_rows, dim), F32),
        pltpu.VMEM((p_rows, dim), F32),
        pltpu.VMEM((p_rows, 2 * dim), BF16),
        pltpu.VMEM((dim, p_rows), BF16),
        pltpu.VMEM((width, q_rows), BF16),
        pltpu.VMEM((16, q_rows, dim), BF16),
        pltpu.VMEM((16, p_rows, q_rows), BF16),
        pltpu.VMEM((16, passages, q_rows), F32),
        pltpu.VMEM((q_rows, 128), F32),
        pltpu.VMEM((q_rows, 128), BF16),
        pltpu.VMEM((16, passages, q_rows), F32),
        pltpu.VMEM((p_rows, dim), F32),
        pltpu.VMEM((16, 8, 128), F32),
        pltpu.VMEM((128, 128), F32),
        pltpu.VMEM((passages, 128), F32),
        pltpu.VMEM((passages, 128), F32),
        pltpu.VMEM((passages, 128), F32),
        pltpu.VMEM((8, 128), F32),
        pltpu.VMEM((16, 8, 128), F32),
        pltpu.VMEM((32, 128), F32),
        pltpu.VMEM((8, 128), F32),
        pltpu.VMEM((16, dim, q_rows), BF16),
        pltpu.VMEM((8, dim, q_rows), BF16),
        pltpu.VMEM((8, dim, q_rows), BF16),
        pltpu.VMEM((2, dim, q_rows), F32),
        pltpu.VMEM((8, dim, q_rows), BF16),
        pltpu.VMEM((dim, q_rows), BF16),
        pltpu.VMEM((dim, q_rows), BF16),
        pltpu.VMEM((p_rows, dim), BF16),
        pltpu.VMEM((dim, p_rows), BF16),
        pltpu.VMEM((q_rows, dim), BF16),
        pltpu.VMEM((width, dim), F32),
        pltpu.VMEM((32, piece, dim), BF16),
        pltpu.VMEM((32, piece, dim), BF16),
        pltpu.VMEM((piece, dim), BF16),
        pltpu.VMEM((8, piece, dim), BF16),
        pltpu.VMEM((32, piece, dim), BF16),
        pltpu.SemaphoreType.DMA((SEND.total,)),
        pltpu.SemaphoreType.DMA((RECV.total,)),
        pltpu.SemaphoreType.DMA((LOCAL.total,)),
    ]
    losses, total, query_grad, passage_grad = pl.pallas_call(
        kernel,
        out_shape=(
            pltpu.VMEM((8, 128), F32),
            pltpu.VMEM((width, dim), F32),
            pltpu.VMEM((q_rows, width), BF16),
            pltpu.VMEM((p_rows, width), BF16),
        ),
        in_specs=[smem, smem, hbm, hbm, hbm, vmem],
        out_specs=(vmem, vmem, vmem, vmem),
        scratch_shapes=scratch,
        compiler_params=pltpu.CompilerParams(
            collective_id=0, has_side_effects=True, vmem_limit_bytes=60 << 20
        ),
        name="late_interaction_step",
    )(
        passage_len,
        positive,
        query_hidden.reshape(q_rows, width),
        passage_hidden.reshape(p_rows, width),
        projection,
        hard_ids,
    )
    losses, grad_proj, grad_query, grad_passage = pl.pallas_call(
        write_out,
        out_shape=(
            jax.ShapeDtypeStruct((queries,), F32),
            jax.ShapeDtypeStruct((width, dim), F32),
            jax.ShapeDtypeStruct((q_rows, width), BF16),
            jax.ShapeDtypeStruct((p_rows, width), BF16),
        ),
        in_specs=[vmem] * 4,
        out_specs=(smem, hbm, hbm, hbm),
        scratch_shapes=[pltpu.SemaphoreType.DMA((2 + OUT_CHUNKS,))],
        compiler_params=pltpu.CompilerParams(vmem_limit_bytes=1 << 20),
        name="write_out",
    )(losses, total, query_grad, passage_grad)
    return (
        losses,
        grad_proj,
        grad_query.reshape(query_hidden.shape),
        grad_passage.reshape(passage_hidden.shape),
    )


def solution(mesh):
    split = Mesh(mesh.devices.reshape(2, 4, 2, 4, 4), AXES)
    placed = (
        P(SPLIT, None, None),
        P(SPLIT, None, None),
        P(),
        P(SPLIT),
        P(SPLIT, None),
        P(SPLIT),
    )
    return jax.shard_map(
        local,
        mesh=split,
        in_specs=placed,
        out_specs=(P(SPLIT), P(), P(SPLIT, None, None), P(SPLIT, None, None)),
        check_vma=False,
    )
```

```python
import functools

import jax
import jax.numpy as jnp
from jax import lax
from jax.experimental import pallas as pl
from jax.experimental.pallas import tpu as pltpu
from jax.sharding import Mesh
from jax.sharding import PartitionSpec as P

MESH = pl.DeviceIdType.MESH
F32 = jnp.float32
BF16 = jnp.bfloat16

AXES = ("zh", "x", "c", "zl", "y")
SPLIT = ("zl", "y", "zh", "x", "c")
norm_eps = 1e-06
EXP2_SCALE = 14.426950408889634
SHIFT = 12.0
HIGHEST = lax.Precision.HIGHEST

GROUP_RELATIVE = [(dz, dx, dc) for dz in range(2) for dx in range(4) for dc in range(2)]

PLANE_RELATIVE = [(dx, dc, dy) for dx in range(4) for dc in range(2) for dy in range(4)]

PLANE_FAR_FIRST = sorted(
    PLANE_RELATIVE[1:], key=lambda r: (-min(r[0], 4 - r[0]) - min(r[2], 4 - r[2]), r)
)


def slot_of(dz, dx, dc):
    return dz * 8 + dx * 2 + dc


def back(d, n):
    return (n - d) % n


def contract_last(left, right):
    return lax.dot_general(
        left, right, (((1,), (1,)), ((), ())), preferred_element_type=F32
    )


def norm_vjp(pre, grad):
    scale = lax.rsqrt(jnp.sum(pre * pre, axis=-1, keepdims=True) + norm_eps)
    along = jnp.sum(pre * grad, axis=-1, keepdims=True)
    return scale * grad - pre * (scale * scale * scale * along)


class Sems:
    def __init__(self):
        self.total = 0

    def take(self, count):
        first = self.total
        self.total += count
        return first


SEND = Sems()
RECV = Sems()
LOCAL = Sems()
S_GATHER, R_GATHER = SEND.take(11), RECV.take(16)
S_HALF, R_HALF = SEND.take(8), RECV.take(32)
S_STATS, R_STATS = SEND.take(16), RECV.take(16)
S_HARD, R_HARD = SEND.take(32), RECV.take(32)
S_HZ, R_HZ = SEND.take(8), RECV.take(8)
S_QC, R_QC = SEND.take(8), RECV.take(8)
S_QX, R_QX = SEND.take(8), RECV.take(8)
S_QZ, R_QZ = SEND.take(1), RECV.take(1)
S_RP, R_RP = SEND.take(32), RECV.take(32)
S_AZ, R_AZ = SEND.take(8), RECV.take(8)
S_GP, R_GP = SEND.take(32), RECV.take(32)
P_CHUNKS = 4
FSTEP = 4
BSTEP = 4
OUT_CHUNKS = 8
L_IN = LOCAL.take(P_CHUNKS)
L_QUERY, L_PROJ, L_SMALL = LOCAL.take(1), LOCAL.take(1), LOCAL.take(3)


def kernel(
    plen_hbm,
    positive_hbm,
    query_hbm,
    passage_hbm,
    projection_hbm,
    hard_ids_hbm,
    losses_out,
    total_out,
    gq_out,
    gp_out,
    plen,
    positive,
    hard_ids,
    query_hidden,
    projection,
    ph,
    q_pre,
    p_pre,
    pe,
    pe_t,
    qh_t,
    qg,
    e_ref,
    sums,
    spread_from,
    one_lane,
    w_ref,
    pg,
    meta,
    meta_rows,
    counts_ref,
    chosen_ref,
    score_ref,
    st_send,
    st_recv,
    h_recv,
    hz_recv,
    qgt,
    rc,
    cs,
    own_c,
    rx,
    zs,
    rz,
    pb_ref,
    pb_t,
    qb_ref,
    w_loc,
    w_send,
    rp_recv,
    h_send,
    az_recv,
    parts,
    ssem,
    rsem,
    lsem,
    entry,
):
    zh, x, c = lax.axis_index("zh"), lax.axis_index("x"), lax.axis_index("c")
    zl, y = lax.axis_index("zl"), lax.axis_index("y")
    z = zh * 4 + zl

    def at_x(d):
        return {"x": lax.rem(x + d, 4)}

    def at_y(d):
        return {"y": lax.rem(y + d, 4)}

    def at_z(d):
        there = lax.rem(z + d, 8)
        return {"zh": there // 4, "zl": lax.rem(there, 4)}

    def in_group(dz, dx, dc):
        return {"zh": lax.rem(zh + dz, 2), "x": lax.rem(x + dx, 4), "c": lax.rem(c + dc, 2)}

    def in_plane(dx, dc, dy):
        return {"x": lax.rem(x + dx, 4), "c": lax.rem(c + dc, 2), "y": lax.rem(y + dy, 4)}

    partner = {"c": 1 - c}
    across = {"zh": 1 - zh}

    def group_of(dz, dx, dc):
        return (lax.rem(zh + dz, 2) * 4 + lax.rem(x + dx, 4)) * 2 + lax.rem(c + dc, 2)

    def push(src, dst, s, r, device):
        pltpu.make_async_remote_copy(
            src_ref=src,
            dst_ref=dst,
            send_sem=ssem.at[s],
            recv_sem=rsem.at[r],
            device_id=device,
            device_id_type=MESH,
        ).start()

    def arrived(dst, r):
        pltpu.make_async_remote_copy(
            src_ref=dst,
            dst_ref=dst,
            send_sem=ssem.at[0],
            recv_sem=rsem.at[r],
            device_id=partner,
            device_id_type=MESH,
        ).wait_recv()

    def sent(src, s):
        pltpu.make_async_remote_copy(
            src_ref=src,
            dst_ref=src,
            send_sem=ssem.at[s],
            recv_sem=rsem.at[0],
            device_id=partner,
            device_id_type=MESH,
        ).wait_send()

    rows_in = ph.shape[0] // P_CHUNKS

    def load(k):
        at = pl.ds(k * rows_in, rows_in)
        return pltpu.make_async_copy(passage_hbm.at[at], ph.at[at], lsem.at[L_IN + k])

    load_query = pltpu.make_async_copy(query_hbm, query_hidden, lsem.at[L_QUERY])
    load_proj = pltpu.make_async_copy(projection_hbm, projection, lsem.at[L_PROJ])
    small = [
        pltpu.make_async_copy(src, dst, lsem.at[L_SMALL + n])
        for n, (src, dst) in enumerate(
            ((plen_hbm, plen), (positive_hbm, positive), (hard_ids_hbm, hard_ids))
        )
    ]
    load_query.start()
    load_proj.start()
    for copy in small:
        copy.start()
    for k in range(P_CHUNKS):
        load(k).start()

    barrier = pltpu.get_barrier_semaphore()
    peers = [partner]
    peers += [at_x(d) for d in range(1, 4)]
    peers += [at_y(d) for d in range(1, 4)]
    peers += [at_z(d) for d in range(1, 8)]
    for peer in peers:
        pl.semaphore_signal(barrier, inc=1, device_id=peer, device_id_type=MESH)

    load_query.wait()
    load_proj.wait()
    pre = jnp.dot(query_hidden[...], projection[...], preferred_element_type=F32)
    q_pre[...] = pre
    scale = lax.rsqrt(jnp.sum(pre * pre, axis=-1, keepdims=True) + norm_eps)
    qg[0, 0:256] = (pre * scale).astype(BF16)

    lanes = lax.broadcasted_iota(jnp.int32, (8, 128), 1)
    rows = lax.broadcasted_iota(jnp.int32, (8, 128), 0)
    for copy in small:
        copy.wait()
    chosen_row = jnp.zeros((8, 128), F32)
    for k in range(8):
        chosen_row = jnp.where(rows == k, positive[k].astype(F32), chosen_row)
    meta[0:8, :] = jnp.where(lanes == 32, chosen_row, 0.0)
    meta[8:16, :] = jnp.zeros((8, 128), F32)
    meta[0:8, 0:32] = hard_ids[...].astype(F32)
    qg[0, 256:272] = meta[...].astype(BF16)

    pl.semaphore_wait(barrier, len(peers))
    for d in range(1, 4):
        pl.semaphore_signal(entry.at[0], inc=1, device_id=at_x(d), device_id_type=MESH)

    def half_of(slot, h):
        return qg.at[slot, pl.ds(h * 128, 144 if h else 128)]

    far = slot_of(1, 0, 0)
    for h in range(2):
        push(half_of(0, h), half_of(far, h), S_HALF + h, R_HALF + 2 * far + h, across)
    for n, d in enumerate((2, 1, 3)):
        to = slot_of(0, back(d, 4), 0)
        push(qg.at[0], qg.at[to], S_GATHER + 1 + n, R_GATHER + to, at_x(d))
    push(qg.at[0], qg.at[1], S_GATHER + 4, R_GATHER + 1, partner)
    first_lane = lax.broadcasted_iota(jnp.int32, (128, 128), 1) == 0
    token = lax.broadcasted_iota(jnp.int32, (128, 128), 0)
    for p in range(plen.shape[0]):
        padding = first_lane & (token >= plen[p])
        pe[p * 128 : (p + 1) * 128, 128:256] = jnp.where(padding, -100.0, 0.0).astype(BF16)
    one_lane[...] = (lax.broadcasted_iota(jnp.int32, one_lane.shape, 1) == 0).astype(BF16)
    for k in range(P_CHUNKS):
        load(k).wait()
        at = pl.ds(k * rows_in, rows_in)
        pre = jnp.dot(ph[at, :], projection[...], preferred_element_type=F32)
        p_pre[at, :] = pre
        scale = lax.rsqrt(jnp.sum(pre * pre, axis=-1, keepdims=True) + norm_eps)
        unit = (pre * scale).astype(BF16)
        pe[at, 0:128] = unit
        pe_t[:, at] = unit.T
    qh_t[...] = query_hidden[...].T

    def relay_x(dz, first):
        for n, d in enumerate((1, 2, 3)):
            here, there = slot_of(dz, d, 0), slot_of(dz, d, 1)
            if dz:
                for h in range(2):
                    arrived(half_of(here, h), R_HALF + 2 * here + h)
            else:
                arrived(qg.at[here], R_GATHER + here)
            push(qg.at[here], qg.at[there], first + n, R_GATHER + there, partner)

    def relay_z():
        for h in range(2):
            arrived(half_of(far, h), R_HALF + 2 * far + h)
            for n, d in enumerate((2, 1, 3)):
                to = slot_of(1, back(d, 4), 0)
                push(
                    half_of(far, h),
                    half_of(to, h),
                    S_HALF + 2 + 3 * h + n,
                    R_HALF + 2 * to + h,
                    at_x(d),
                )
        push(qg.at[far], qg.at[far + 1], S_GATHER, R_GATHER + far + 1, partner)

    def count_hard():
        for dz, dx, dc in GROUP_RELATIVE:
            first = pl.multiple_of(group_of(dz, dx, dc) * 8, 8)
            meta_rows[pl.ds(first, 8), :] = qg[slot_of(dz, dx, dc), 256:272].astype(F32)[0:8]
        turned = meta_rows[...].T
        own = (
            group_of(0, 0, 0) * 16 + lax.broadcasted_iota(jnp.int32, (16, 128), 0)
        ).astype(F32)
        counts = jnp.zeros((16, 128), F32)
        for k in range(32):
            counts += (turned[k : k + 1, :] == own).astype(F32)
        counts_ref[...] = counts
        chosen_ref[...] = (turned[32:33, :] == own).astype(F32)

    passages = sums.shape[1]
    step = FSTEP
    height = step * 128

    def grow(k):
        block = jnp.concatenate([qg[k, 0:256], one_lane[...]], axis=1)
        for n in range(passages // step):
            similar = contract_last(pe[n * height : (n + 1) * height, :], block)
            grown = jnp.exp2(similar * EXP2_SCALE)
            for i in range(step):
                p = n * step + i
                live = grown[i * 128 : (i + 1) * 128]
                e_ref[k, p * 128 : (p + 1) * 128, :] = live.astype(BF16)
                sums[k, p : p + 1, :] = jnp.sum(live, axis=0, keepdims=True)

    tokens = sums.shape[2]
    spread_from[...] = (
        lax.broadcasted_iota(jnp.int32, (tokens, 128), 0) // 32
        == lax.rem(lax.broadcasted_iota(jnp.int32, (tokens, 128), 1), 8)
    ).astype(F32)
    lane_group = lax.broadcasted_iota(jnp.int32, (passages, 128), 1) // 8

    def score(t):
        pair = sums[pl.ds(2 * t, 2)].reshape(2 * passages, tokens)
        part = jnp.dot(
            0.1 * jnp.log(pair),
            spread_from[...],
            precision=HIGHEST,
            preferred_element_type=F32,
        )
        first = group_of(t // 4, lax.rem(t, 4), 0)
        second = group_of(t // 4, lax.rem(t, 4), 1)
        score_ref[...] += jnp.where(lane_group == first, part[:passages], 0.0) + jnp.where(
            lane_group == second, part[passages:], 0.0
        )

    score_ref[...] = jnp.zeros_like(score_ref)
    grow(0)
    pl.semaphore_wait(entry.at[0], 3)
    pl.semaphore_signal(entry.at[1], inc=1, device_id=partner, device_id_type=MESH)
    relay_x(0, S_GATHER + 5)
    arrived(qg.at[1], R_GATHER + 1)
    grow(1)

    def forward(t, carry):
        @pl.when(t == 1)
        def _():
            relay_z()

        @pl.when(t == 5)
        def _():
            relay_x(1, S_GATHER + 8)

        arrived(qg.at[2 * t + 1], R_GATHER + 2 * t + 1)

        @pl.when(t == 7)
        def _():
            count_hard()

        score(t - 1)
        grow(2 * t)
        grow(2 * t + 1)
        return carry

    lax.fori_loop(1, 8, forward, 0)

    score(7)
    scores = score_ref[...]
    spread_to = (
        lax.broadcasted_iota(jnp.int32, (128, tokens), 1) // 32
        == lax.rem(lax.broadcasted_iota(jnp.int32, (128, tokens), 0), 8)
    ).astype(F32)
    pl.semaphore_wait(entry.at[1], 1)
    counts, chosen = counts_ref[...], chosen_ref[...]
    grown = jnp.exp(scores - SHIFT)
    hard = counts * grown
    other_hard = jnp.where(chosen > 0.5, 0.0, hard)
    st_send[...] = jnp.zeros_like(st_send)
    st_send[0:1, :] = jnp.sum(grown, axis=0, keepdims=True)
    st_send[1:2, :] = jnp.sum(other_hard * grown, axis=0, keepdims=True)
    st_send[2:3, :] = jnp.sum(chosen * scores, axis=0, keepdims=True)
    h_recv[0:1, :] = jnp.sum(hard, axis=0, keepdims=True)
    own = h_recv.at[pl.ds(0, 1)]
    for dx, dc, dy in PLANE_FAR_FIRST:
        at = dx * 8 + dc * 4 + dy
        to = back(dx, 4) * 8 + dc * 4 + back(dy, 4)
        push(own, h_recv.at[pl.ds(to, 1)], S_HARD + at, R_HARD + to, in_plane(dx, dc, dy))
    for dz, dx, dc in GROUP_RELATIVE[1:]:
        to = slot_of(dz, back(dx, 4), dc)
        push(
            st_send,
            st_recv.at[to],
            S_STATS + slot_of(dz, dx, dc),
            R_STATS + to,
            in_group(dz, dx, dc),
        )
    w_ref[...] = 1.0 / sums[...]
    pg[...] = jnp.zeros_like(pg)
    for n in range(1, 32):
        arrived(h_recv.at[pl.ds(n, 1)], R_HARD + n)
    hz_recv[0:1, :] = jnp.sum(h_recv[...], axis=0, keepdims=True)
    own = hz_recv.at[pl.ds(0, 1)]
    for d in (4, 3, 5, 2, 6, 1, 7):
        push(own, hz_recv.at[pl.ds(8 - d, 1)], S_HZ + d, R_HZ + 8 - d, at_z(d))
    stats = st_send[...]
    for slot in range(1, 16):
        arrived(st_recv.at[slot], R_STATS + slot)
        stats += st_recv[slot]
    for n in range(1, 8):
        arrived(hz_recv.at[pl.ds(n, 1)], R_HZ + n)
    total = jnp.sum(hz_recv[...], axis=0, keepdims=True)
    boost = (8.0 * 65536.0) / jnp.sum(total, axis=1, keepdims=True)
    partition = stats[0:1, :] + boost * stats[1:2, :]
    loss = jnp.log(partition) + SHIFT - stats[2:3, :]
    own_lane = lanes == group_of(0, 0, 0) * 8 + rows
    losses_out[...] = jnp.broadcast_to(
        jnp.sum(jnp.where(own_lane, loss, 0.0), axis=1, keepdims=True), (8, 128)
    )
    score_grad = grown * (1.0 + boost * other_hard) / partition - chosen

    picked = [
        jnp.where(lane_group == group_of(dz, dx, dc), score_grad, 0.0)
        for dz, dx, dc in GROUP_RELATIVE
    ]
    spread = jnp.dot(
        jnp.concatenate(picked, axis=0),
        spread_to,
        precision=HIGHEST,
        preferred_element_type=F32,
    )
    w_ref[...] *= spread.reshape(w_ref.shape)

    def combine(j):
        arrived(rc.at[j], R_QC + j)
        both = qgt[2 * j + 1].astype(F32) + rc[j].astype(F32)
        side = j // 4
        d = lax.rem(j + 1, 4)

        @pl.when(d != 0)
        def _():
            cs[j] = both.astype(BF16)
            to = side * 4 + (4 - d)
            push(cs.at[j], rx.at[to], S_QX + j, R_QX + to, {"x": lax.rem(x + d, 4)})

        @pl.when(d == 0)
        def _():
            own_c[side] = both

    def over_x(side):
        whole = own_c[side]
        for d in range(1, 4):
            arrived(rx.at[side * 4 + d], R_QX + side * 4 + d)
            whole += rx[side * 4 + d].astype(F32)
        return whole

    def backward(j, carry):
        dz = 1 - j // 4
        k = dz * 8 + lax.rem(j + 1, 4) * 2
        both = qg[pl.ds(k, 2), 0:256].reshape(2 * tokens, qg.shape[2])
        acc = None
        for n in range(passages // BSTEP):
            if n == 2:

                @pl.when(j >= 1)
                def _():
                    combine(j - 1)

            parts = []
            for i in range(BSTEP):
                p = n * BSTEP + i
                pair = [
                    (
                        e_ref[k + m, p * 128 : (p + 1) * 128, :].astype(F32)
                        * w_ref[k + m, p : p + 1, :]
                    ).astype(BF16)
                    for m in range(2)
                ]
                parts.append(jnp.concatenate(pair, axis=1))
            coefficient = jnp.concatenate(parts, axis=0) if BSTEP > 1 else parts[0]
            at = slice(n * BSTEP * 128, (n + 1) * BSTEP * 128)
            pg[at, :] += jnp.dot(coefficient, both, preferred_element_type=F32)
            term = jnp.dot(pe_t[:, at], coefficient, preferred_element_type=F32)
            acc = term if acc is None else acc + term
        qgt[2 * j] = acc[:, tokens:].astype(BF16)
        push(qgt.at[2 * j], rc.at[j], S_QC + j, R_QC + j, partner)
        qgt[2 * j + 1] = acc[:, :tokens].astype(BF16)

        @pl.when(j == 5)
        def _():
            zs[...] = over_x(0).astype(BF16)
            push(zs, rz, S_QZ, R_QZ, across)

        return carry

    lax.fori_loop(0, 8, backward, 0)

    for k in range(P_CHUNKS):
        at = pl.ds(k * rows_in, rows_in)
        pb = norm_vjp(p_pre[at, :], pg[at, :]).astype(BF16)
        pb_t[:, at] = pb.T
        pb_ref[at, :] = pb
    w_t = jnp.dot(pb_t[...], ph[...], preferred_element_type=F32)
    w_loc[...] = w_t.T

    combine(7)
    arrived(rz, R_QZ)
    whole = over_x(1) + rz[...].astype(F32)
    qb = norm_vjp(q_pre[...], whole.T).astype(BF16)
    qb_ref[...] = qb
    whole = w_loc[...] + jnp.dot(qh_t[...], qb, preferred_element_type=F32)
    w_loc[...] = whole

    piece = h_send.shape[0]
    for k in range(32):
        w_send[k] = whole[k * piece : (k + 1) * piece].astype(BF16)
    here = (c * 4 + x) * 4 + y
    for dx, dc, dy in PLANE_FAR_FIRST:
        at = dx * 8 + dc * 4 + dy
        to = back(dx, 4) * 8 + dc * 4 + back(dy, 4)
        there = (lax.rem(c + dc, 2) * 4 + lax.rem(x + dx, 4)) * 4 + lax.rem(y + dy, 4)
        push(w_send.at[there], rp_recv.at[to], S_RP + at, R_RP + to, in_plane(dx, dc, dy))
    gq_out[...] = contract_last(qb_ref[...], projection[...]).astype(BF16)
    for k in range(P_CHUNKS):
        at = pl.ds(k * rows_in, rows_in)
        gp_out[at, :] = contract_last(pb_ref[at, :], projection[...]).astype(BF16)
    mine = w_loc[pl.ds(pl.multiple_of(here * piece, 8), piece), :]
    for n in range(1, 32):
        arrived(rp_recv.at[n], R_RP + n)
        mine += rp_recv[n].astype(F32)
    h_send[...] = mine.astype(BF16)
    for d in (4, 3, 5, 2, 6, 1, 7):
        push(h_send, az_recv.at[z], S_AZ + d, R_AZ + 8 - d, at_z(d))
    az_recv[z] = h_send[...]
    for d in range(1, 8):
        arrived(az_recv.at[0], R_AZ + d)
    mine = az_recv[0].astype(F32)
    for k in range(1, 8):
        mine += az_recv[k].astype(F32)
    parts[here] = mine.astype(BF16)
    for dx, dc, dy in PLANE_FAR_FIRST:
        at = dx * 8 + dc * 4 + dy
        to = back(dx, 4) * 8 + dc * 4 + back(dy, 4)
        push(parts.at[here], parts.at[here], S_GP + at, R_GP + to, in_plane(dx, dc, dy))
    for n in range(1, 32):
        arrived(parts.at[0], R_GP + n)
    piece = total_out.shape[0] // 32
    for k in range(32):
        total_out[k * piece : (k + 1) * piece, :] = parts[k].astype(F32)

    for n in range(11):
        sent(qg.at[0], S_GATHER + n)
    for n in range(8):
        sent(half_of(0, 0 if n in (0, 2, 3, 4) else 1), S_HALF + n)
    for n in range(1, 16):
        sent(st_send, S_STATS + n)
    for n in range(1, 32):
        sent(h_recv.at[pl.ds(0, 1)], S_HARD + n)
    for n in range(1, 8):
        sent(hz_recv.at[pl.ds(0, 1)], S_HZ + n)
    for n in range(8):
        sent(qgt.at[0], S_QC + n)
        if n % 4 != 3:
            sent(cs.at[0], S_QX + n)
    sent(zs, S_QZ)
    for n in range(1, 32):
        sent(w_send.at[0], S_RP + n)
        sent(parts.at[0], S_GP + n)
    for d in range(1, 8):
        sent(h_send, S_AZ + d)


def write_out(losses, total, gq, gp, losses_out, total_hbm, gq_hbm, gp_hbm, sem):
    rows = gp.shape[0] // OUT_CHUNKS
    copies = []
    for k in range(OUT_CHUNKS):
        at = pl.ds(k * rows, rows)
        copies.append((gp.at[at], gp_hbm.at[at]))
    copies += [(gq, gq_hbm), (total, total_hbm)]
    copies = [pltpu.make_async_copy(a, b, sem.at[n]) for n, (a, b) in enumerate(copies)]
    for copy in copies:
        copy.start()
    for k in range(losses_out.shape[0]):
        losses_out[k] = jnp.sum(losses[k : k + 1, 0:1])
    for copy in copies:
        copy.wait()


def local(query_hidden, passage_hidden, projection, positive, hard_ids, passage_len):
    queries, query_len, width = query_hidden.shape
    passages, slots, _ = passage_hidden.shape
    dim = projection.shape[1]
    q_rows, p_rows = queries * query_len, passages * slots
    piece = width // 32
    vmem = pl.BlockSpec(memory_space=pltpu.VMEM)
    smem = pl.BlockSpec(memory_space=pltpu.SMEM)
    hbm = pl.BlockSpec(memory_space=pl.ANY)
    scratch = [
        pltpu.SMEM(passage_len.shape, jnp.int32),
        pltpu.SMEM(positive.shape, jnp.int32),
        pltpu.VMEM(hard_ids.shape, jnp.int32),
        pltpu.VMEM((q_rows, width), BF16),
        pltpu.VMEM((width, dim), BF16),
        pltpu.VMEM((p_rows, width), BF16),
        pltpu.VMEM((q_rows, dim), F32),
        pltpu.VMEM((p_rows, dim), F32),
        pltpu.VMEM((p_rows, 2 * dim), BF16),
        pltpu.VMEM((dim, p_rows), BF16),
        pltpu.VMEM((width, q_rows), BF16),
        pltpu.VMEM((16, q_rows + 16, dim), BF16),
        pltpu.VMEM((16, p_rows, q_rows), BF16),
        pltpu.VMEM((16, passages, q_rows), F32),
        pltpu.VMEM((q_rows, 128), F32),
        pltpu.VMEM((q_rows, 128), BF16),
        pltpu.VMEM((16, passages, q_rows), F32),
        pltpu.VMEM((p_rows, dim), F32),
        pltpu.VMEM((16, 128), F32),
        pltpu.VMEM((128, 128), F32),
        pltpu.VMEM((passages, 128), F32),
        pltpu.VMEM((passages, 128), F32),
        pltpu.VMEM((passages, 128), F32),
        pltpu.VMEM((8, 128), F32),
        pltpu.VMEM((16, 8, 128), F32),
        pltpu.VMEM((32, 128), F32),
        pltpu.VMEM((8, 128), F32),
        pltpu.VMEM((16, dim, q_rows), BF16),
        pltpu.VMEM((8, dim, q_rows), BF16),
        pltpu.VMEM((8, dim, q_rows), BF16),
        pltpu.VMEM((2, dim, q_rows), F32),
        pltpu.VMEM((8, dim, q_rows), BF16),
        pltpu.VMEM((dim, q_rows), BF16),
        pltpu.VMEM((dim, q_rows), BF16),
        pltpu.VMEM((p_rows, dim), BF16),
        pltpu.VMEM((dim, p_rows), BF16),
        pltpu.VMEM((q_rows, dim), BF16),
        pltpu.VMEM((width, dim), F32),
        pltpu.VMEM((32, piece, dim), BF16),
        pltpu.VMEM((32, piece, dim), BF16),
        pltpu.VMEM((piece, dim), BF16),
        pltpu.VMEM((8, piece, dim), BF16),
        pltpu.VMEM((32, piece, dim), BF16),
        pltpu.SemaphoreType.DMA((SEND.total,)),
        pltpu.SemaphoreType.DMA((RECV.total,)),
        pltpu.SemaphoreType.DMA((LOCAL.total,)),
        pltpu.SemaphoreType.REGULAR((2,)),
    ]
    losses, total, query_grad, passage_grad = pl.pallas_call(
        kernel,
        out_shape=(
            pltpu.VMEM((8, 128), F32),
            pltpu.VMEM((width, dim), F32),
            pltpu.VMEM((q_rows, width), BF16),
            pltpu.VMEM((p_rows, width), BF16),
        ),
        in_specs=[hbm] * 6,
        out_specs=(vmem, vmem, vmem, vmem),
        scratch_shapes=scratch,
        compiler_params=pltpu.CompilerParams(
            collective_id=0, has_side_effects=True, vmem_limit_bytes=60 << 20
        ),
        name="late_interaction_step",
    )(
        passage_len,
        positive,
        query_hidden.reshape(q_rows, width),
        passage_hidden.reshape(p_rows, width),
        projection,
        hard_ids,
    )
    losses, grad_proj, grad_query, grad_passage = pl.pallas_call(
        write_out,
        out_shape=(
            jax.ShapeDtypeStruct((queries,), F32),
            jax.ShapeDtypeStruct((width, dim), F32),
            jax.ShapeDtypeStruct((q_rows, width), BF16),
            jax.ShapeDtypeStruct((p_rows, width), BF16),
        ),
        in_specs=[vmem] * 4,
        out_specs=(smem, hbm, hbm, hbm),
        scratch_shapes=[pltpu.SemaphoreType.DMA((2 + OUT_CHUNKS,))],
        compiler_params=pltpu.CompilerParams(vmem_limit_bytes=1 << 20),
        name="write_out",
    )(losses, total, query_grad, passage_grad)
    return (
        losses,
        grad_proj,
        grad_query.reshape(query_hidden.shape),
        grad_passage.reshape(passage_hidden.shape),
    )


def solution(mesh):
    split = Mesh(mesh.devices.reshape(2, 4, 2, 4, 4), AXES)
    placed = (
        P(SPLIT, None, None),
        P(SPLIT, None, None),
        P(),
        P(SPLIT),
        P(SPLIT, None),
        P(SPLIT),
    )
    return jax.shard_map(
        local,
        mesh=split,
        in_specs=placed,
        out_specs=(P(SPLIT), P(), P(SPLIT, None, None), P(SPLIT, None, None)),
        check_vma=False,
    )
```

```python
import functools

import jax
import jax.numpy as jnp
from jax import lax
from jax.experimental import pallas as pl
from jax.experimental.pallas import tpu as pltpu
from jax.sharding import Mesh
from jax.sharding import PartitionSpec as P

MESH = pl.DeviceIdType.MESH
F32 = jnp.float32
BF16 = jnp.bfloat16

AXES = ("zh", "x", "c", "zl", "y")
SPLIT = ("zl", "y", "zh", "x", "c")
norm_eps = 1e-06
EXP2_SCALE = 14.426950408889634
SHIFT = 12.0
HIGHEST = lax.Precision.HIGHEST

GROUP_RELATIVE = [(dz, dx, dc) for dz in range(2) for dx in range(4) for dc in range(2)]

PLANE_RELATIVE = [(dx, dc, dy) for dx in range(4) for dc in range(2) for dy in range(4)]

PLANE_FAR_FIRST = sorted(
    PLANE_RELATIVE[1:], key=lambda r: (-min(r[0], 4 - r[0]) - min(r[2], 4 - r[2]), r)
)


def slot_of(dz, dx, dc):
    return dz * 8 + dx * 2 + dc


def back(d, n):
    return (n - d) % n


def contract_last(left, right):
    return lax.dot_general(
        left, right, (((1,), (1,)), ((), ())), preferred_element_type=F32
    )


def norm_vjp(pre, grad):
    scale = lax.rsqrt(jnp.sum(pre * pre, axis=-1, keepdims=True) + norm_eps)
    along = jnp.sum(pre * grad, axis=-1, keepdims=True)
    return scale * grad - pre * (scale * scale * scale * along)


class Sems:
    def __init__(self):
        self.total = 0

    def take(self, count):
        first = self.total
        self.total += count
        return first


SEND = Sems()
RECV = Sems()
LOCAL = Sems()
S_GATHER, R_GATHER = SEND.take(11), RECV.take(16)
S_HALF, R_HALF = SEND.take(8), RECV.take(32)
S_STATS, R_STATS = SEND.take(16), RECV.take(16)
S_HARD, R_HARD = SEND.take(32), RECV.take(32)
S_HZ, R_HZ = SEND.take(8), RECV.take(8)
S_QC, R_QC = SEND.take(8), RECV.take(8)
S_QX, R_QX = SEND.take(8), RECV.take(8)
S_QZ, R_QZ = SEND.take(1), RECV.take(1)
S_RP, R_RP = SEND.take(32), RECV.take(32)
S_AZ, R_AZ = SEND.take(8), RECV.take(8)
S_GP, R_GP = SEND.take(32), RECV.take(32)
P_CHUNKS = 4
FSTEP = 4
BSTEP = 4
OUT_CHUNKS = 8
L_IN = LOCAL.take(P_CHUNKS)
L_QUERY, L_PROJ, L_SMALL = LOCAL.take(1), LOCAL.take(1), LOCAL.take(3)


def kernel(
    plen_hbm,
    positive_hbm,
    query_hbm,
    passage_hbm,
    projection_hbm,
    hard_ids_hbm,
    losses_out,
    total_out,
    gq_out,
    gp_out,
    plen,
    positive,
    hard_ids,
    query_hidden,
    projection,
    ph,
    q_pre,
    p_pre,
    pe,
    pe_t,
    qh_t,
    qg,
    e_ref,
    sums,
    spread_from,
    one_lane,
    w_ref,
    pg,
    meta,
    meta_rows,
    counts_ref,
    chosen_ref,
    score_ref,
    st_send,
    st_recv,
    h_recv,
    hz_recv,
    qgt,
    rc,
    cs,
    own_c,
    rx,
    zs,
    rz,
    pb_ref,
    pb_t,
    qb_ref,
    w_loc,
    w_send,
    rp_recv,
    h_send,
    az_recv,
    parts,
    ssem,
    rsem,
    lsem,
    entry,
):
    zh, x, c = lax.axis_index("zh"), lax.axis_index("x"), lax.axis_index("c")
    zl, y = lax.axis_index("zl"), lax.axis_index("y")
    z = zh * 4 + zl

    def at_x(d):
        return {"x": lax.rem(x + d, 4)}

    def at_y(d):
        return {"y": lax.rem(y + d, 4)}

    def at_z(d):
        there = lax.rem(z + d, 8)
        return {"zh": there // 4, "zl": lax.rem(there, 4)}

    def in_group(dz, dx, dc):
        return {"zh": lax.rem(zh + dz, 2), "x": lax.rem(x + dx, 4), "c": lax.rem(c + dc, 2)}

    def in_plane(dx, dc, dy):
        return {"x": lax.rem(x + dx, 4), "c": lax.rem(c + dc, 2), "y": lax.rem(y + dy, 4)}

    partner = {"c": 1 - c}
    across = {"zh": 1 - zh}

    def group_of(dz, dx, dc):
        return (lax.rem(zh + dz, 2) * 4 + lax.rem(x + dx, 4)) * 2 + lax.rem(c + dc, 2)

    def push(src, dst, s, r, device):
        pltpu.make_async_remote_copy(
            src_ref=src,
            dst_ref=dst,
            send_sem=ssem.at[s],
            recv_sem=rsem.at[r],
            device_id=device,
            device_id_type=MESH,
        ).start()

    def arrived(dst, r):
        pltpu.make_async_remote_copy(
            src_ref=dst,
            dst_ref=dst,
            send_sem=ssem.at[0],
            recv_sem=rsem.at[r],
            device_id=partner,
            device_id_type=MESH,
        ).wait_recv()

    def sent(src, s):
        pltpu.make_async_remote_copy(
            src_ref=src,
            dst_ref=src,
            send_sem=ssem.at[s],
            recv_sem=rsem.at[0],
            device_id=partner,
            device_id_type=MESH,
        ).wait_send()

    rows_in = ph.shape[0] // P_CHUNKS

    def load(k):
        at = pl.ds(k * rows_in, rows_in)
        return pltpu.make_async_copy(passage_hbm.at[at], ph.at[at], lsem.at[L_IN + k])

    load_query = pltpu.make_async_copy(query_hbm, query_hidden, lsem.at[L_QUERY])
    load_proj = pltpu.make_async_copy(projection_hbm, projection, lsem.at[L_PROJ])
    small = [
        pltpu.make_async_copy(src, dst, lsem.at[L_SMALL + n])
        for n, (src, dst) in enumerate(
            ((plen_hbm, plen), (positive_hbm, positive), (hard_ids_hbm, hard_ids))
        )
    ]
    load_query.start()
    load_proj.start()
    for copy in small:
        copy.start()
    for k in range(P_CHUNKS):
        load(k).start()

    barrier = pltpu.get_barrier_semaphore()
    peers = [partner]
    peers += [at_x(d) for d in range(1, 4)]
    peers += [at_y(d) for d in range(1, 4)]
    peers += [at_z(d) for d in range(1, 8)]
    for peer in peers:
        pl.semaphore_signal(barrier, inc=1, device_id=peer, device_id_type=MESH)

    load_query.wait()
    load_proj.wait()
    pre = jnp.dot(query_hidden[...], projection[...], preferred_element_type=F32)
    q_pre[...] = pre
    scale = lax.rsqrt(jnp.sum(pre * pre, axis=-1, keepdims=True) + norm_eps)
    qg[0, 0:256] = (pre * scale).astype(BF16)

    lanes = lax.broadcasted_iota(jnp.int32, (8, 128), 1)
    rows = lax.broadcasted_iota(jnp.int32, (8, 128), 0)
    for copy in small:
        copy.wait()
    chosen_row = jnp.zeros((8, 128), F32)
    for k in range(8):
        chosen_row = jnp.where(rows == k, positive[k].astype(F32), chosen_row)
    meta[0:8, :] = jnp.where(lanes == 32, chosen_row, 0.0)
    meta[8:16, :] = jnp.zeros((8, 128), F32)
    meta[0:8, 0:32] = hard_ids[...].astype(F32)
    qg[0, 256:272] = meta[...].astype(BF16)

    pl.semaphore_wait(barrier, len(peers))
    for d in range(1, 4):
        pl.semaphore_signal(entry.at[0], inc=1, device_id=at_x(d), device_id_type=MESH)

    def half_of(slot, h):
        return qg.at[slot, pl.ds(h * 128, 144 if h else 128)]

    far = slot_of(1, 0, 0)
    for h in range(2):
        push(half_of(0, h), half_of(far, h), S_HALF + h, R_HALF + 2 * far + h, across)
    for n, d in enumerate((2, 1, 3)):
        to = slot_of(0, back(d, 4), 0)
        push(qg.at[0], qg.at[to], S_GATHER + 1 + n, R_GATHER + to, at_x(d))
    push(qg.at[0], qg.at[1], S_GATHER + 4, R_GATHER + 1, partner)
    first_lane = lax.broadcasted_iota(jnp.int32, (128, 128), 1) == 0
    token = lax.broadcasted_iota(jnp.int32, (128, 128), 0)
    for p in range(plen.shape[0]):
        padding = first_lane & (token >= plen[p])
        pe[p * 128 : (p + 1) * 128, 128:256] = jnp.where(padding, -100.0, 0.0).astype(BF16)
    one_lane[...] = (lax.broadcasted_iota(jnp.int32, one_lane.shape, 1) == 0).astype(BF16)
    for k in range(P_CHUNKS):
        load(k).wait()
        at = pl.ds(k * rows_in, rows_in)
        pre = jnp.dot(ph[at, :], projection[...], preferred_element_type=F32)
        p_pre[at, :] = pre
        scale = lax.rsqrt(jnp.sum(pre * pre, axis=-1, keepdims=True) + norm_eps)
        unit = (pre * scale).astype(BF16)
        pe[at, 0:128] = unit
        pe_t[:, at] = unit.T
    qh_t[...] = query_hidden[...].T

    def relay_x(dz, first):
        for n, d in enumerate((1, 2, 3)):
            here, there = slot_of(dz, d, 0), slot_of(dz, d, 1)
            if dz:
                for h in range(2):
                    arrived(half_of(here, h), R_HALF + 2 * here + h)
            else:
                arrived(qg.at[here], R_GATHER + here)
            push(qg.at[here], qg.at[there], first + n, R_GATHER + there, partner)

    def relay_z(h):
        arrived(half_of(far, h), R_HALF + 2 * far + h)
        for n, d in enumerate((2, 1, 3)):
            to = slot_of(1, back(d, 4), 0)
            push(
                half_of(far, h),
                half_of(to, h),
                S_HALF + 2 + 3 * h + n,
                R_HALF + 2 * to + h,
                at_x(d),
            )
        if h:
            push(qg.at[far], qg.at[far + 1], S_GATHER, R_GATHER + far + 1, partner)

    def count_hard():
        for dz, dx, dc in GROUP_RELATIVE:
            first = pl.multiple_of(group_of(dz, dx, dc) * 8, 8)
            meta_rows[pl.ds(first, 8), :] = qg[slot_of(dz, dx, dc), 256:272].astype(F32)[0:8]
        turned = meta_rows[...].T
        own = (
            group_of(0, 0, 0) * 16 + lax.broadcasted_iota(jnp.int32, (16, 128), 0)
        ).astype(F32)
        counts = jnp.zeros((16, 128), F32)
        for k in range(32):
            counts += (turned[k : k + 1, :] == own).astype(F32)
        counts_ref[...] = counts
        chosen_ref[...] = (turned[32:33, :] == own).astype(F32)

    passages = sums.shape[1]
    step = FSTEP
    height = step * 128

    def grow(k):
        block = jnp.concatenate([qg[k, 0:256], one_lane[...]], axis=1)
        for n in range(passages // step):
            similar = contract_last(pe[n * height : (n + 1) * height, :], block)
            grown = jnp.exp2(similar * EXP2_SCALE)
            for i in range(step):
                p = n * step + i
                live = grown[i * 128 : (i + 1) * 128]
                e_ref[k, p * 128 : (p + 1) * 128, :] = live.astype(BF16)
                sums[k, p : p + 1, :] = jnp.sum(live, axis=0, keepdims=True)

    tokens = sums.shape[2]
    spread_from[...] = (
        lax.broadcasted_iota(jnp.int32, (tokens, 128), 0) // 32
        == lax.rem(lax.broadcasted_iota(jnp.int32, (tokens, 128), 1), 8)
    ).astype(F32)
    lane_group = lax.broadcasted_iota(jnp.int32, (passages, 128), 1) // 8

    def score(t):
        pair = sums[pl.ds(2 * t, 2)].reshape(2 * passages, tokens)
        part = jnp.dot(
            0.1 * jnp.log(pair),
            spread_from[...],
            precision=HIGHEST,
            preferred_element_type=F32,
        )
        first = group_of(t // 4, lax.rem(t, 4), 0)
        second = group_of(t // 4, lax.rem(t, 4), 1)
        score_ref[...] += jnp.where(lane_group == first, part[:passages], 0.0) + jnp.where(
            lane_group == second, part[passages:], 0.0
        )

    score_ref[...] = jnp.zeros_like(score_ref)
    grow(0)
    pl.semaphore_wait(entry.at[0], 3)
    pl.semaphore_signal(entry.at[1], inc=1, device_id=partner, device_id_type=MESH)
    relay_x(0, S_GATHER + 5)
    arrived(qg.at[1], R_GATHER + 1)
    grow(1)

    def forward(t, carry):
        @pl.when(t == 1)
        def _():
            relay_z(0)

        @pl.when(t == 2)
        def _():
            relay_z(1)

        @pl.when(t == 5)
        def _():
            relay_x(1, S_GATHER + 8)

        arrived(qg.at[2 * t + 1], R_GATHER + 2 * t + 1)

        @pl.when(t == 7)
        def _():
            count_hard()

        score(t - 1)
        grow(2 * t)
        grow(2 * t + 1)
        return carry

    lax.fori_loop(1, 8, forward, 0)

    score(7)
    scores = score_ref[...]
    spread_to = (
        lax.broadcasted_iota(jnp.int32, (128, tokens), 1) // 32
        == lax.rem(lax.broadcasted_iota(jnp.int32, (128, tokens), 0), 8)
    ).astype(F32)
    pl.semaphore_wait(entry.at[1], 1)
    counts, chosen = counts_ref[...], chosen_ref[...]
    grown = jnp.exp(scores - SHIFT)
    hard = counts * grown
    other_hard = jnp.where(chosen > 0.5, 0.0, hard)
    st_send[...] = jnp.zeros_like(st_send)
    st_send[0:1, :] = jnp.sum(grown, axis=0, keepdims=True)
    st_send[1:2, :] = jnp.sum(other_hard * grown, axis=0, keepdims=True)
    st_send[2:3, :] = jnp.sum(chosen * scores, axis=0, keepdims=True)
    h_recv[0:1, :] = jnp.sum(hard, axis=0, keepdims=True)
    own = h_recv.at[pl.ds(0, 1)]
    for dx, dc, dy in PLANE_FAR_FIRST:
        at = dx * 8 + dc * 4 + dy
        to = back(dx, 4) * 8 + dc * 4 + back(dy, 4)
        push(own, h_recv.at[pl.ds(to, 1)], S_HARD + at, R_HARD + to, in_plane(dx, dc, dy))
    for dz, dx, dc in GROUP_RELATIVE[1:]:
        to = slot_of(dz, back(dx, 4), dc)
        push(
            st_send,
            st_recv.at[to],
            S_STATS + slot_of(dz, dx, dc),
            R_STATS + to,
            in_group(dz, dx, dc),
        )
    w_ref[...] = 1.0 / sums[...]
    pg[...] = jnp.zeros_like(pg)
    for n in range(1, 32):
        arrived(h_recv.at[pl.ds(n, 1)], R_HARD + n)
    hz_recv[0:1, :] = jnp.sum(h_recv[...], axis=0, keepdims=True)
    own = hz_recv.at[pl.ds(0, 1)]
    for d in (4, 3, 5, 2, 6, 1, 7):
        push(own, hz_recv.at[pl.ds(8 - d, 1)], S_HZ + d, R_HZ + 8 - d, at_z(d))
    stats = st_send[...]
    for slot in range(1, 16):
        arrived(st_recv.at[slot], R_STATS + slot)
        stats += st_recv[slot]
    for n in range(1, 8):
        arrived(hz_recv.at[pl.ds(n, 1)], R_HZ + n)
    total = jnp.sum(hz_recv[...], axis=0, keepdims=True)
    boost = (8.0 * 65536.0) / jnp.sum(total, axis=1, keepdims=True)
    partition = stats[0:1, :] + boost * stats[1:2, :]
    loss = jnp.log(partition) + SHIFT - stats[2:3, :]
    own_lane = lanes == group_of(0, 0, 0) * 8 + rows
    losses_out[...] = jnp.broadcast_to(
        jnp.sum(jnp.where(own_lane, loss, 0.0), axis=1, keepdims=True), (8, 128)
    )
    score_grad = grown * (1.0 + boost * other_hard) / partition - chosen

    picked = [
        jnp.where(lane_group == group_of(dz, dx, dc), score_grad, 0.0)
        for dz, dx, dc in GROUP_RELATIVE
    ]
    spread = jnp.dot(
        jnp.concatenate(picked, axis=0),
        spread_to,
        precision=HIGHEST,
        preferred_element_type=F32,
    )
    w_ref[...] *= spread.reshape(w_ref.shape)

    def combine(j):
        arrived(rc.at[j], R_QC + j)
        both = qgt[2 * j + 1].astype(F32) + rc[j].astype(F32)
        side = j // 4
        d = lax.rem(j + 1, 4)

        @pl.when(d != 0)
        def _():
            cs[j] = both.astype(BF16)
            to = side * 4 + (4 - d)
            push(cs.at[j], rx.at[to], S_QX + j, R_QX + to, {"x": lax.rem(x + d, 4)})

        @pl.when(d == 0)
        def _():
            own_c[side] = both

    def over_x(side):
        whole = own_c[side]
        for d in range(1, 4):
            arrived(rx.at[side * 4 + d], R_QX + side * 4 + d)
            whole += rx[side * 4 + d].astype(F32)
        return whole

    def backward(j, carry):
        dz = 1 - j // 4
        k = dz * 8 + lax.rem(j + 1, 4) * 2
        both = qg[pl.ds(k, 2), 0:256].reshape(2 * tokens, qg.shape[2])
        acc = None
        for n in range(passages // BSTEP):
            parts = []
            for i in range(BSTEP):
                p = n * BSTEP + i
                pair = [
                    (
                        e_ref[k + m, p * 128 : (p + 1) * 128, :].astype(F32)
                        * w_ref[k + m, p : p + 1, :]
                    ).astype(BF16)
                    for m in range(2)
                ]
                parts.append(jnp.concatenate(pair, axis=1))
            coefficient = jnp.concatenate(parts, axis=0) if BSTEP > 1 else parts[0]
            at = slice(n * BSTEP * 128, (n + 1) * BSTEP * 128)
            pg[at, :] += jnp.dot(coefficient, both, preferred_element_type=F32)
            term = jnp.dot(pe_t[:, at], coefficient, preferred_element_type=F32)
            acc = term if acc is None else acc + term
        qgt[2 * j] = acc[:, tokens:].astype(BF16)
        push(qgt.at[2 * j], rc.at[j], S_QC + j, R_QC + j, partner)
        qgt[2 * j + 1] = acc[:, :tokens].astype(BF16)

        @pl.when(j >= 1)
        def _():
            combine(j - 1)

        @pl.when(j == 5)
        def _():
            zs[...] = over_x(0).astype(BF16)
            push(zs, rz, S_QZ, R_QZ, across)

        return carry

    lax.fori_loop(0, 8, backward, 0)

    for k in range(P_CHUNKS):
        at = pl.ds(k * rows_in, rows_in)
        pb = norm_vjp(p_pre[at, :], pg[at, :]).astype(BF16)
        pb_t[:, at] = pb.T
        pb_ref[at, :] = pb
    w_t = jnp.dot(pb_t[...], ph[...], preferred_element_type=F32)
    w_loc[...] = w_t.T

    combine(7)
    arrived(rz, R_QZ)
    whole = over_x(1) + rz[...].astype(F32)
    qb = norm_vjp(q_pre[...], whole.T).astype(BF16)
    qb_ref[...] = qb
    whole = w_loc[...] + jnp.dot(qh_t[...], qb, preferred_element_type=F32)
    w_loc[...] = whole

    piece = h_send.shape[0]
    for k in range(32):
        w_send[k] = whole[k * piece : (k + 1) * piece].astype(BF16)
    here = (c * 4 + x) * 4 + y
    for dx, dc, dy in PLANE_FAR_FIRST:
        at = dx * 8 + dc * 4 + dy
        to = back(dx, 4) * 8 + dc * 4 + back(dy, 4)
        there = (lax.rem(c + dc, 2) * 4 + lax.rem(x + dx, 4)) * 4 + lax.rem(y + dy, 4)
        push(w_send.at[there], rp_recv.at[to], S_RP + at, R_RP + to, in_plane(dx, dc, dy))
    gq_out[...] = contract_last(qb_ref[...], projection[...]).astype(BF16)
    for k in range(P_CHUNKS):
        at = pl.ds(k * rows_in, rows_in)
        gp_out[at, :] = contract_last(pb_ref[at, :], projection[...]).astype(BF16)
    mine = w_loc[pl.ds(pl.multiple_of(here * piece, 8), piece), :]
    for n in range(1, 32):
        arrived(rp_recv.at[n], R_RP + n)
        mine += rp_recv[n].astype(F32)
    h_send[...] = mine.astype(BF16)
    for d in (4, 3, 5, 2, 6, 1, 7):
        push(h_send, az_recv.at[z], S_AZ + d, R_AZ + 8 - d, at_z(d))
    az_recv[z] = h_send[...]
    for d in range(1, 8):
        arrived(az_recv.at[0], R_AZ + d)
    mine = az_recv[0].astype(F32)
    for k in range(1, 8):
        mine += az_recv[k].astype(F32)
    parts[here] = mine.astype(BF16)
    for dx, dc, dy in PLANE_FAR_FIRST:
        at = dx * 8 + dc * 4 + dy
        to = back(dx, 4) * 8 + dc * 4 + back(dy, 4)
        push(parts.at[here], parts.at[here], S_GP + at, R_GP + to, in_plane(dx, dc, dy))
    for n in range(1, 32):
        arrived(parts.at[0], R_GP + n)
    piece = total_out.shape[0] // 32
    for k in range(32):
        total_out[k * piece : (k + 1) * piece, :] = parts[k].astype(F32)

    for n in range(11):
        sent(qg.at[0], S_GATHER + n)
    for n in range(8):
        sent(half_of(0, 0 if n in (0, 2, 3, 4) else 1), S_HALF + n)
    for n in range(1, 16):
        sent(st_send, S_STATS + n)
    for n in range(1, 32):
        sent(h_recv.at[pl.ds(0, 1)], S_HARD + n)
    for n in range(1, 8):
        sent(hz_recv.at[pl.ds(0, 1)], S_HZ + n)
    for n in range(8):
        sent(qgt.at[0], S_QC + n)
        if n % 4 != 3:
            sent(cs.at[0], S_QX + n)
    sent(zs, S_QZ)
    for n in range(1, 32):
        sent(w_send.at[0], S_RP + n)
        sent(parts.at[0], S_GP + n)
    for d in range(1, 8):
        sent(h_send, S_AZ + d)


def write_out(losses, total, gq, gp, losses_out, total_hbm, gq_hbm, gp_hbm, sem):
    rows = gp.shape[0] // OUT_CHUNKS
    copies = []
    for k in range(OUT_CHUNKS):
        at = pl.ds(k * rows, rows)
        copies.append((gp.at[at], gp_hbm.at[at]))
    copies += [(gq, gq_hbm), (total, total_hbm)]
    copies = [pltpu.make_async_copy(a, b, sem.at[n]) for n, (a, b) in enumerate(copies)]
    for copy in copies:
        copy.start()
    for k in range(losses_out.shape[0]):
        losses_out[k] = jnp.sum(losses[k : k + 1, 0:1])
    for copy in copies:
        copy.wait()


def local(query_hidden, passage_hidden, projection, positive, hard_ids, passage_len):
    queries, query_len, width = query_hidden.shape
    passages, slots, _ = passage_hidden.shape
    dim = projection.shape[1]
    q_rows, p_rows = queries * query_len, passages * slots
    piece = width // 32
    vmem = pl.BlockSpec(memory_space=pltpu.VMEM)
    smem = pl.BlockSpec(memory_space=pltpu.SMEM)
    hbm = pl.BlockSpec(memory_space=pl.ANY)
    scratch = [
        pltpu.SMEM(passage_len.shape, jnp.int32),
        pltpu.SMEM(positive.shape, jnp.int32),
        pltpu.VMEM(hard_ids.shape, jnp.int32),
        pltpu.VMEM((q_rows, width), BF16),
        pltpu.VMEM((width, dim), BF16),
        pltpu.VMEM((p_rows, width), BF16),
        pltpu.VMEM((q_rows, dim), F32),
        pltpu.VMEM((p_rows, dim), F32),
        pltpu.VMEM((p_rows, 2 * dim), BF16),
        pltpu.VMEM((dim, p_rows), BF16),
        pltpu.VMEM((width, q_rows), BF16),
        pltpu.VMEM((16, q_rows + 16, dim), BF16),
        pltpu.VMEM((16, p_rows, q_rows), BF16),
        pltpu.VMEM((16, passages, q_rows), F32),
        pltpu.VMEM((q_rows, 128), F32),
        pltpu.VMEM((q_rows, 128), BF16),
        pltpu.VMEM((16, passages, q_rows), F32),
        pltpu.VMEM((p_rows, dim), F32),
        pltpu.VMEM((16, 128), F32),
        pltpu.VMEM((128, 128), F32),
        pltpu.VMEM((passages, 128), F32),
        pltpu.VMEM((passages, 128), F32),
        pltpu.VMEM((passages, 128), F32),
        pltpu.VMEM((8, 128), F32),
        pltpu.VMEM((16, 8, 128), F32),
        pltpu.VMEM((32, 128), F32),
        pltpu.VMEM((8, 128), F32),
        pltpu.VMEM((16, dim, q_rows), BF16),
        pltpu.VMEM((8, dim, q_rows), BF16),
        pltpu.VMEM((8, dim, q_rows), BF16),
        pltpu.VMEM((2, dim, q_rows), F32),
        pltpu.VMEM((8, dim, q_rows), BF16),
        pltpu.VMEM((dim, q_rows), BF16),
        pltpu.VMEM((dim, q_rows), BF16),
        pltpu.VMEM((p_rows, dim), BF16),
        pltpu.VMEM((dim, p_rows), BF16),
        pltpu.VMEM((q_rows, dim), BF16),
        pltpu.VMEM((width, dim), F32),
        pltpu.VMEM((32, piece, dim), BF16),
        pltpu.VMEM((32, piece, dim), BF16),
        pltpu.VMEM((piece, dim), BF16),
        pltpu.VMEM((8, piece, dim), BF16),
        pltpu.VMEM((32, piece, dim), BF16),
        pltpu.SemaphoreType.DMA((SEND.total,)),
        pltpu.SemaphoreType.DMA((RECV.total,)),
        pltpu.SemaphoreType.DMA((LOCAL.total,)),
        pltpu.SemaphoreType.REGULAR((2,)),
    ]
    losses, total, query_grad, passage_grad = pl.pallas_call(
        kernel,
        out_shape=(
            pltpu.VMEM((8, 128), F32),
            pltpu.VMEM((width, dim), F32),
            pltpu.VMEM((q_rows, width), BF16),
            pltpu.VMEM((p_rows, width), BF16),
        ),
        in_specs=[hbm] * 6,
        out_specs=(vmem, vmem, vmem, vmem),
        scratch_shapes=scratch,
        compiler_params=pltpu.CompilerParams(
            collective_id=0, has_side_effects=True, vmem_limit_bytes=60 << 20
        ),
        name="late_interaction_step",
    )(
        passage_len,
        positive,
        query_hidden.reshape(q_rows, width),
        passage_hidden.reshape(p_rows, width),
        projection,
        hard_ids,
    )
    losses, grad_proj, grad_query, grad_passage = pl.pallas_call(
        write_out,
        out_shape=(
            jax.ShapeDtypeStruct((queries,), F32),
            jax.ShapeDtypeStruct((width, dim), F32),
            jax.ShapeDtypeStruct((q_rows, width), BF16),
            jax.ShapeDtypeStruct((p_rows, width), BF16),
        ),
        in_specs=[vmem] * 4,
        out_specs=(smem, hbm, hbm, hbm),
        scratch_shapes=[pltpu.SemaphoreType.DMA((2 + OUT_CHUNKS,))],
        compiler_params=pltpu.CompilerParams(vmem_limit_bytes=1 << 20),
        name="write_out",
    )(losses, total, query_grad, passage_grad)
    return (
        losses,
        grad_proj,
        grad_query.reshape(query_hidden.shape),
        grad_passage.reshape(passage_hidden.shape),
    )


def solution(mesh):
    split = Mesh(mesh.devices.reshape(2, 4, 2, 4, 4), AXES)
    placed = (
        P(SPLIT, None, None),
        P(SPLIT, None, None),
        P(),
        P(SPLIT),
        P(SPLIT, None),
        P(SPLIT),
    )
    return jax.shard_map(
        local,
        mesh=split,
        in_specs=placed,
        out_specs=(P(SPLIT), P(), P(SPLIT, None, None), P(SPLIT, None, None)),
        check_vma=False,
    )
```
